256 devices in a mesh: node: 128 (over x, z, y), rel: 2 (over core).
Axes of the slice: x: 4, y: 4, z: 8, core: 2. Of those that a mesh axis runs over, the one named last changes fastest.
Arguments:
- node_state: bfloat16 [65536, 128], P('node'), may hold values from -6 to 6
- send_list: int32 [128, 128], P('node'), may hold values from 0 to 3
- tile_weight: bfloat16 [128, 2, 192, 128, 128], P('node', 'rel'), may hold values from -0.078125 to 0.078125
- tile_slot: int32 [128, 2, 192], P('node', 'rel'), may hold values from 0 to 127
- tile_dst: int32 [128, 2, 192], P('node', 'rel'), may hold values from 0 to 3
- tile_rel: int32 [128, 2, 192], P('node', 'rel'), may hold values from 0 to 534
- live_groups: int32 [128, 2], P('node', 'rel'), may hold values from 1 to 12, as said below
- query_rel: int32 [4], replicated, may hold values from 0 to 534
- query_head: int32 [4], replicated, may hold values from 0 to 65535
- rel_table: float32 [535, 32], replicated, may hold values from -6 to 6
- rel_proj: bfloat16 [2, 32, 17120], replicated, may hold values from -1 to 1
- upd_weight: float32 [2, 32, 32], replicated, may hold values from -1 to 1
- cotangent: bfloat16 [65536, 128], P('node'), may hold values from -6 to 6
Outputs:
- final_state: bfloat16 [65536, 128], P('node')
- grad_state: float32 [65536, 128], P('node')
- grad_proj: bfloat16 [2, 32, 17120], replicated
- grad_upd: float32 [2, 32, 32], replicated
The draws below stay inside these ranges and needn't reach their ends.
Inputs may be any that keep to these rules, and one draw needn't show every extreme that they name: `live_groups`: of the two devices of one chip, one has more than 6 live groups and the other 6 or fewer; some device has all 12.
All inputs are finite; a program needn't handle non-finite values.
Results may differ from the reference program's by a relative error of at most 0.009.
Values may be sent and summed in bfloat16 or wider, within the bound.
No kernel may reach another device: no remote copies, remote signals or barrier semaphores. Data moves between devices by JAX's collectives and lax.ppermute only.
A program may use at most 128 MiB of HBM per device.

```python
import jax
import jax.numpy as jnp
from jax import lax

H = 32
R = 535
BLK = 128
Q = 4
L = 2
GROUP = 16
GROUPS = 12
NB_DEV = 4
COLS = 128
TILES = 192
HALF = 6
NODES = 65536
N_NODE = 128


def draw_live_groups(key, part):
    keys = jax.random.split(key, 4)
    big_counts = jax.random.randint(keys[0], (N_NODE,), HALF + 1, GROUPS + 1)
    small_counts = jax.random.randint(keys[1], (N_NODE,), 1, HALF + 1)
    full_chip = jax.random.randint(keys[2], (), 0, N_NODE)
    chip_ids = jnp.arange(N_NODE, dtype=jnp.int32)
    big_counts = jnp.where(chip_ids == full_chip, GROUPS, big_counts)
    flipped = jax.random.randint(keys[3], (N_NODE,), 0, 2)
    first_core = jnp.where(flipped == 1, big_counts, small_counts)
    second_core = jnp.where(flipped == 1, small_counts, big_counts)
    return jnp.stack([first_core, second_core], axis=1).astype(jnp.int32)


def draw_tile_rel(key, part):
    keys = jax.random.split(jax.random.fold_in(key, 7), 3)
    device_ids = jnp.arange(N_NODE, dtype=jnp.int32)[:, None, None] * 2 + jnp.arange(2, dtype=jnp.int32)[None, :, None]
    own_pick = jax.random.randint(keys[0], (N_NODE, 2, TILES), 0, 2)
    own_rel = (2 * device_ids + own_pick) % R
    spread_rel = jax.random.randint(keys[1], (N_NODE, 2, TILES), 0, R)
    chooser = jax.random.randint(keys[2], (N_NODE, 2, TILES), 0, 4)
    return jnp.where(chooser == 0, spread_rel, own_rel).astype(jnp.int32)


def with_ends(values, key, smallest, top_value):
    longest = values.shape.index(max(values.shape))
    spots = []
    for shift in (0, 1):
        where = [jax.random.randint(jax.random.fold_in(key, axis), (), 0, length) for axis, length in enumerate(values.shape)]
        where[longest] = (where[longest] + shift) % values.shape[longest]
        spots.append(tuple(where))
    return values.at[spots[0]].set(smallest).at[spots[1]].set(top_value)


def level_of(key, shape, pieces, least, top_value):
    level = 1.0
    for axis_at, parts in pieces:
        heights = jax.random.uniform(jax.random.fold_in(jax.random.fold_in(key, 6), axis_at), (parts,), jnp.float32, least / len(pieces), top_value / len(pieces))
        level = level * jnp.repeat(jnp.exp(heights), shape[axis_at] // parts).reshape((-1,) + (1,) * (len(shape) - 1 - axis_at))
    return level


def noise(key, dims, deviation, limit, cuts=(), held_as=jnp.bfloat16):
    loudness = level_of(key, dims, cuts, -0.22, 0.18) if cuts else 1.0
    drawn = jax.random.normal(key, dims, jnp.float32) * deviation * loudness
    return jnp.minimum(jnp.maximum(drawn, -limit), limit).astype(held_as)


def setup_inputs(seed: int = 0) -> dict:
    splits = jax.random.split(jax.random.key(seed), 14)
    node_state = noise(splits[0], (NODES, COLS), 1.0, 6.0, ((0, 128),))
    send_list = with_ends(jax.random.randint(splits[1], (N_NODE, N_NODE), 0, NB_DEV), jax.random.fold_in(splits[1], 1), 0, NB_DEV - 1).astype(jnp.int32)
    tile_weight = noise(splits[2], (N_NODE, 2, TILES, BLK, BLK), (BLK * TILES // NB_DEV) ** -0.5, 0.078125, ((0, 128), (1, 2)))
    tile_slot = with_ends(jax.random.randint(splits[3], (N_NODE, 2, TILES), 0, N_NODE), jax.random.fold_in(splits[3], 1), 0, N_NODE - 1).astype(jnp.int32)
    tile_dst = with_ends(jax.random.randint(splits[4], (N_NODE, 2, TILES), 0, NB_DEV), jax.random.fold_in(splits[4], 1), 0, NB_DEV - 1).astype(jnp.int32)
    tile_rel = draw_tile_rel(jax.random.fold_in(splits[13], 71), 0)
    live_groups = draw_live_groups(jax.random.fold_in(splits[13], 71), 0)
    query_rel = with_ends(jax.random.randint(splits[7], (Q,), 0, R), jax.random.fold_in(splits[7], 1), 0, R - 1).astype(jnp.int32)
    query_head = with_ends(jax.random.randint(splits[8], (Q,), 0, NODES), jax.random.fold_in(splits[8], 1), 0, NODES - 1).astype(jnp.int32)
    rel_table = noise(splits[9], (R, H), 1.0, 6.0, (), jnp.float32)
    rel_proj = noise(splits[10], (L, H, R * H), H ** -0.5, 1.0)
    upd_weight = noise(splits[11], (L, H, H), H ** -0.5, 1.0, (), jnp.float32)
    cotangent = noise(splits[12], (NODES, COLS), 1.0, 6.0, ((0, 128),))
    return {"node_state": node_state, "send_list": send_list, "tile_weight": tile_weight, "tile_slot": tile_slot, "tile_dst": tile_dst, "tile_rel": tile_rel, "live_groups": live_groups, "query_rel": query_rel, "query_head": query_head, "rel_table": rel_table, "rel_proj": rel_proj, "upd_weight": upd_weight, "cotangent": cotangent}


EXACT_MATMUL = lax.Precision.HIGHEST

def relation_vectors(rel_table, query_rel, rel_proj):
    relation_ids = jnp.arange(R, dtype=jnp.int32)
    picked = (query_rel[:, None] == relation_ids[None, :]).astype(jnp.float32)
    query_vec = jnp.dot(picked, rel_table, precision=EXACT_MATMUL)
    tables = []
    for layer_index in range(L):
        flat_rows = jnp.dot(query_vec, rel_proj[layer_index].astype(jnp.float32), precision=EXACT_MATMUL)
        tables.append(flat_rows.reshape(Q, R, H).transpose(1, 0, 2).reshape(R, Q * H))
    return (query_vec, tables)

def boundary_rows(query_vec, query_head, first_row, row_count):
    row_ids = first_row + jnp.arange(row_count, dtype=jnp.int32)
    matches = (row_ids[:, None] == query_head[None, :]).astype(jnp.float32)
    return (matches[:, :, None] * query_vec[None, :, :]).reshape(row_count, Q * H)

def mix_hidden(aggregate, weight):
    row_count = aggregate.shape[0]
    return jnp.einsum('nqh,hk->nqk', aggregate.reshape(row_count, Q, H), weight, precision=EXACT_MATMUL).reshape(row_count, Q * H)

def mix_back(gradient, weight):
    row_count = gradient.shape[0]
    return jnp.einsum('nqk,hk->nqh', gradient.reshape(row_count, Q, H), weight, precision=EXACT_MATMUL).reshape(row_count, Q * H)

def weight_grad(aggregate, gradient):
    row_count = aggregate.shape[0]
    return jnp.einsum('nqh,nqk->hk', aggregate.reshape(row_count, Q, H), gradient.reshape(row_count, Q, H), precision=EXACT_MATMUL)

def silu_slope(hidden_pre):
    sigma = jax.nn.sigmoid(hidden_pre)
    return sigma * (1.0 + hidden_pre * (1.0 - sigma))

def reference(node_state, send_list, tile_weight, tile_slot, tile_dst, tile_rel, live_groups, query_rel, query_head, rel_table, rel_proj, upd_weight, cotangent):
    columns = Q * H
    query_vec, tables = relation_vectors(rel_table, query_rel, rel_proj)
    bound_term = boundary_rows(query_vec, query_head, 0, NODES)
    owners = jnp.arange(N_NODE, dtype=jnp.int32)
    tile_ids = jnp.arange(TILES, dtype=jnp.int32)
    block_ids = jnp.arange(NB_DEV, dtype=jnp.int32)
    relation_ids = jnp.arange(R, dtype=jnp.int32)

    def device_tiles(blocks, target_node_index, core_index, factor_table):
        received = blocks[owners, send_list[:, target_node_index]]
        edge_weight_values = tile_weight[target_node_index, core_index].astype(jnp.float32)
        sources = received[tile_slot[target_node_index, core_index]]
        factors = factor_table[tile_rel[target_node_index, core_index]]
        active_group_mask = (tile_ids < GROUP * live_groups[target_node_index, core_index]).astype(jnp.float32)
        reshape_into_block = (tile_dst[target_node_index, core_index][:, None] == block_ids[None, :]).astype(jnp.float32) * active_group_mask[:, None]
        to_relation = (tile_rel[target_node_index, core_index][:, None] == relation_ids[None, :]).astype(jnp.float32) * active_group_mask[:, None]
        return (edge_weight_values, sources, factors, active_group_mask, reshape_into_block, to_relation)
    history = []
    current = node_state
    for layer_index in range(L):
        factor_table = tables[layer_index]
        blocks = current.reshape(N_NODE, NB_DEV, BLK, columns)

        def forward_node(running_message_sum, target_node_index, blocks=blocks, factor_table=factor_table):
            for core_index in range(2):
                edge_weight_values, sources, factors, active_group_mask, reshape_into_block, to_relation = device_tiles(blocks, target_node_index, core_index, factor_table)
                scaled_messages = lax.optimization_barrier((sources.astype(jnp.float32) * factors[:, None, :]).astype(jnp.bfloat16))
                message_share = jnp.einsum('kvm,kmq->kvq', edge_weight_values, scaled_messages.astype(jnp.float32), precision=EXACT_MATMUL)
                running_message_sum = running_message_sum.at[target_node_index].add(jnp.einsum('xo,xzj->ozj', reshape_into_block, message_share, precision=EXACT_MATMUL))
            return (running_message_sum, None)
        running_message_sum, _ = lax.scan(forward_node, jnp.zeros((N_NODE, NB_DEV, BLK, columns), jnp.float32), owners)
        aggregate = running_message_sum.reshape(NODES, columns) + bound_term
        hidden_pre = mix_hidden(aggregate, upd_weight[layer_index])
        history.append((current, aggregate, hidden_pre))
        current = (current.astype(jnp.float32) + jax.nn.silu(hidden_pre)).astype(jnp.bfloat16)
    scale_factor = float(NODES) ** (-0.5)
    grad_state = cotangent.astype(jnp.float32)
    proj_grads = [None] * L
    upd_grads = [None] * L
    for layer_index in reversed(range(L)):
        previous, aggregate, hidden_pre = history[layer_index]
        factor_table = tables[layer_index]
        blocks = previous.reshape(N_NODE, NB_DEV, BLK, columns)
        grad_pre = grad_state * silu_slope(hidden_pre)
        upd_grads[layer_index] = weight_grad(aggregate, grad_pre) * scale_factor
        grad_agg = mix_back(grad_pre, upd_weight[layer_index]).astype(jnp.bfloat16).reshape(N_NODE, NB_DEV, BLK, columns)

        def backward_node(carried, target_node_index, blocks=blocks, factor_table=factor_table, grad_agg=grad_agg):
            owner_total, relation_total = carried
            for core_index in range(2):
                edge_weight_values, sources, factors, active_group_mask, reshape_into_block, to_relation = device_tiles(blocks, target_node_index, core_index, factor_table)
                inbound_messages = grad_agg[target_node_index][tile_dst[target_node_index, core_index]].astype(jnp.float32)
                source_rows_loaded = jnp.einsum('rwz,rwk->rzk', edge_weight_values, inbound_messages, precision=EXACT_MATMUL) * active_group_mask[:, None, None]
                grad_source = source_rows_loaded * factors[:, None, :]
                slot_total = jnp.zeros((N_NODE, BLK, columns), jnp.float32).at[tile_slot[target_node_index, core_index]].add(grad_source)
                owner_total = owner_total.at[owners, send_list[:, target_node_index]].add(slot_total)
                row_terms = lax.optimization_barrier(jnp.sum(source_rows_loaded * sources.astype(jnp.float32), axis=1))
                relation_total = relation_total + jnp.dot(to_relation.T, row_terms, precision=EXACT_MATMUL)
            return ((owner_total, relation_total), None)
        start_value = (jnp.zeros((N_NODE, NB_DEV, BLK, columns), jnp.float32), jnp.zeros((R, columns), jnp.float32))
        (owner_total, relation_total), _ = lax.scan(backward_node, start_value, owners)
        grad_state = grad_state + owner_total.reshape(NODES, columns)
        proj_grads[layer_index] = jnp.einsum('qh,rqk->hrk', query_vec, relation_total.reshape(R, Q, H), precision=EXACT_MATMUL).reshape(H, R * H) * scale_factor
    return (current, grad_state, jnp.stack(proj_grads).astype(jnp.bfloat16), jnp.stack(upd_grads))
```

```python
import functools

import jax
import jax.numpy as jnp
from jax import lax
from jax.experimental import pallas as pl
from jax.experimental.pallas import tpu as pltpu
from jax.sharding import Mesh
from jax.sharding import PartitionSpec as P

H = 32
R = 535
BLK = 128
HB = BLK // 2
Q = 4
L = 2
GROUP = 16
NB_DEV = 4
COLS = Q * H
ROWS = NB_DEV * HB
R8 = 536
REL_ROWS = R8 + H
F32 = jnp.float32
BF16 = jnp.bfloat16
EXACT_MATMUL = lax.Precision.HIGHEST
VMEM_LIMIT = 48 * 1024 * 1024
SWAP = [(0, 1), (1, 0)]
SMEM_SPEC = pl.BlockSpec(memory_space=pltpu.SMEM)
VMEM_SPEC = pl.BlockSpec(memory_space=pltpu.VMEM)
ANY_SPEC = pl.BlockSpec(memory_space=pl.ANY)


def grid_dims(node_count):
    if node_count == 128:
        return (4, 8, 4)
    return (2, node_count // 4, 2)


def params():
    return pltpu.CompilerParams(vmem_limit_bytes=VMEM_LIMIT)


def relation_vectors(rel_table, query_rel, rel_proj):
    relation_ids = jnp.arange(R, dtype=jnp.int32)
    picked = (query_rel[:, None] == relation_ids[None, :]).astype(F32)
    query_vec = jnp.dot(picked, rel_table, precision=EXACT_MATMUL)
    tables = []
    for layer_index in range(L):
        flat_rows = jnp.dot(
            query_vec, rel_proj[layer_index].astype(F32), precision=EXACT_MATMUL
        )
        table = flat_rows.reshape(Q, R, H).transpose(1, 0, 2).reshape(R, COLS)
        tables.append(jnp.pad(table, ((0, R8 - R), (0, 0))))
    return (query_vec, tables)


def split_kernel(pos, w_ref, f_keep, f_send, b_keep, b_send):
    core = pos[3]
    own = pl.multiple_of(core * HB, HB)
    other = pl.multiple_of((1 - core) * HB, HB)
    f_keep[...] = w_ref[:, pl.ds(own, HB), :]
    f_send[...] = w_ref[:, pl.ds(other, HB), :]
    for t in range(w_ref.shape[0]):
        flipped = w_ref[t].T
        low, high = flipped[:HB], flipped[HB:]
        b_keep[t] = jnp.where(core == 0, low, high)
        b_send[t] = jnp.where(core == 0, high, low)


def split_weights(pos, weights):
    tiles = weights.shape[0]
    half = jax.ShapeDtypeStruct((tiles, HB, BLK), BF16)
    spec = pl.BlockSpec((GROUP, HB, BLK), lambda g: (g, 0, 0))
    return pl.pallas_call(
        split_kernel,
        out_shape=(half,) * 4,
        grid=(tiles // GROUP,),
        in_specs=[SMEM_SPEC, pl.BlockSpec((GROUP, BLK, BLK), lambda g: (g, 0, 0))],
        out_specs=[spec] * 4,
        compiler_params=params(),
        cost_estimate=pl.CostEstimate(
            flops=0, bytes_accessed=tiles * BLK * BLK * 2 * 3, transcendentals=0
        ),
        name="split_weights",
    )(pos, weights)


def provide_kernel(dims, pos, sends, *refs):
    nx, nz, ny = dims
    pieces, out = refs[:nz], refs[nz]
    z = pos[1]
    nodes = nx * nz * ny
    for k in range(nz):
        owner = lax.rem(z - k + nz, nz)
        for d in range(nx * ny):
            reader = (d // ny) * (nz * ny) + z * ny + d % ny
            block = sends[k * nodes + reader]
            start = pl.multiple_of(block * HB, HB)
            out[d, owner] = pieces[k][pl.ds(start, HB), :]


def provide(dims, pos, sends, pieces):
    nx, nz, ny = dims
    return pl.pallas_call(
        functools.partial(provide_kernel, dims),
        out_shape=jax.ShapeDtypeStruct((nx * ny, nz, HB, COLS), BF16),
        in_specs=[SMEM_SPEC, SMEM_SPEC] + [VMEM_SPEC] * nz,
        out_specs=VMEM_SPEC,
        compiler_params=params(),
        name="provide",
    )(pos, sends, *pieces)


def start_weights(meta, tiles, weights, buffer, sems):
    groups = tiles // GROUP
    for source in range(2):
        live = meta[(source * 4 + 3) * tiles]
        for g in range(groups):

            @pl.when(g < live)
            def _(source=source, g=g):
                pltpu.make_async_copy(
                    weights[source].at[pl.ds(g * GROUP, GROUP)],
                    buffer.at[source * groups + g],
                    sems.at[source * groups + g],
                ).start()


def over_tiles(meta, tiles, weights, buffer, sems, one_tile):
    groups = tiles // GROUP
    for source in range(2):
        live = meta[(source * 4 + 3) * tiles]
        base = source * 4 * tiles

        def one_group(g, carry, source=source, base=base):
            place = source * groups + g
            pltpu.make_async_copy(
                weights[source].at[pl.ds(g * GROUP, GROUP)],
                buffer.at[place],
                sems.at[place],
            ).wait()
            for t in range(GROUP):
                at = base + g * GROUP + t
                one_tile(
                    buffer[place, t],
                    meta[at],
                    meta[at + tiles],
                    meta[at + 2 * tiles],
                )
            return carry

        lax.fori_loop(0, live, one_group, 0)


def update_terms(aggregate, grad_pre, block_mask):
    product = jnp.dot(aggregate.T, grad_pre, precision=EXACT_MATMUL, preferred_element_type=F32)
    product = product * block_mask
    total = product[:H]
    for q in range(1, Q):
        total = total + product[q * H : (q + 1) * H]
    return total


def before_backward(grad, pre, aggregate, upd_t, block_mask, gagg_ref, upd_ref):
    sigma = jax.nn.sigmoid(pre)
    grad_pre = grad * (sigma * (1.0 + pre * (1.0 - sigma)))
    gagg_ref[...] = jnp.dot(
        grad_pre, upd_t, precision=EXACT_MATMUL, preferred_element_type=F32
    ).astype(BF16)
    upd_ref[...] = update_terms(aggregate, grad_pre, block_mask)


def forward_kernel(last, tiles, meta, pos, rec_own, rec_other, w_own, w_other, table, bound,
                   upd, state, *refs):
    if last:
        cotangent, upd_t, block_mask = refs[:3]
        next_ref, gagg_ref, upd_ref, rec, buffer, acc, w_sems, r_sems = refs[3:]
    else:
        next_ref, agg_ref, pre_ref, rec, buffer, acc, w_sems, r_sems = refs
    own = pl.multiple_of(pos[3] * HB, HB)
    other = pl.multiple_of((1 - pos[3]) * HB, HB)
    copies = [
        pltpu.make_async_copy(rec_own, rec.at[:, pl.ds(own, HB), :], r_sems.at[0]),
        pltpu.make_async_copy(rec_other, rec.at[:, pl.ds(other, HB), :], r_sems.at[1]),
    ]
    for copy in copies:
        copy.start()
    start_weights(meta, tiles, (w_own, w_other), buffer, w_sems)
    acc[...] = jnp.zeros_like(acc)
    for copy in copies:
        copy.wait()

    def one_tile(weight, slot, dst, rel):
        message = jnp.dot(weight, rec[slot], preferred_element_type=F32)
        acc[dst] = acc[dst] + message * table[pl.ds(rel, 1), :]

    over_tiles(meta, tiles, (w_own, w_other), buffer, w_sems, one_tile)
    aggregate = acc[...].reshape(ROWS, COLS) + bound[...]
    pre = jnp.dot(aggregate, upd[...], precision=EXACT_MATMUL, preferred_element_type=F32)
    next_ref[...] = (state[...].astype(F32) + pre * jax.nn.sigmoid(pre)).astype(BF16)
    if last:
        before_backward(
            cotangent[...].astype(F32), pre, aggregate, upd_t[...], block_mask[...],
            gagg_ref, upd_ref,
        )
    else:
        agg_ref[...] = aggregate
        pre_ref[...] = pre


def forward(last, meta, pos, rec_own, rec_other, w_own, w_other, table, bound, upd, state, more):
    slots, tiles = rec_own.shape[0], w_own.shape[0]
    places = 2 * (tiles // GROUP)
    rows16 = jax.ShapeDtypeStruct((ROWS, COLS), BF16)
    rows32 = jax.ShapeDtypeStruct((ROWS, COLS), F32)
    if last:
        outs = (rows16, rows16, jax.ShapeDtypeStruct((H, COLS), F32))
    else:
        outs = (rows16, rows32, rows32)
    return pl.pallas_call(
        functools.partial(forward_kernel, last, tiles),
        out_shape=outs,
        in_specs=[SMEM_SPEC, SMEM_SPEC] + [ANY_SPEC] * 4 + [VMEM_SPEC] * (4 + len(more)),
        out_specs=(VMEM_SPEC,) * 3,
        scratch_shapes=[
            pltpu.VMEM((slots, BLK, COLS), BF16),
            pltpu.VMEM((places, GROUP, HB, BLK), BF16),
            pltpu.VMEM((NB_DEV, HB, COLS), F32),
            pltpu.SemaphoreType.DMA((places,)),
            pltpu.SemaphoreType.DMA((2,)),
        ],
        compiler_params=params(),
        name="forward_last" if last else "forward_first",
    )(meta, pos, rec_own, rec_other, w_own, w_other, table, bound, upd, state, *more)


def backward_kernel(dims, tiles, chunk, meta, pos, rec_own, w_own, w_other, gagg_own,
                    gagg_other, table, upd_sum, out, rec, buffer, slot_acc, rel_acc, gagg,
                    w_sems, r_sem):
    nx, nz, ny = dims
    copy = pltpu.make_async_copy(rec_own, rec, r_sem.at[0])
    copy.start()
    start_weights(meta, tiles, (w_own, w_other), buffer, w_sems)
    own = pl.multiple_of(pos[3] * HB, HB)
    other = pl.multiple_of((1 - pos[3]) * HB, HB)
    gagg[:, pl.ds(own, HB), :] = gagg_own[...].reshape(NB_DEV, HB, COLS)
    gagg[:, pl.ds(other, HB), :] = gagg_other[...].reshape(NB_DEV, HB, COLS)
    rel_acc[...] = jnp.zeros_like(rel_acc)
    rel_acc[R8 : R8 + H, :] = upd_sum[...]

    def clear(d, carry):
        slot_acc[pl.ds(d * nz, nz)] = jnp.zeros((nz, HB, COLS), F32)
        return carry

    lax.fori_loop(0, nx * ny, clear, 0)
    copy.wait()

    def one_tile(weight, slot, dst, rel):
        back = jnp.dot(weight, gagg[dst], preferred_element_type=F32)
        row = pl.ds(rel, 1)
        slot_acc[slot] = slot_acc[slot] + back * table[row, :]
        terms = jnp.sum(back * rec[slot].astype(F32), axis=0, keepdims=True)
        rel_acc[row, :] = rel_acc[row, :] + terms

    over_tiles(meta, tiles, (w_own, w_other), buffer, w_sems, one_tile)

    def put(d, carry):
        out[d, : nz * HB, :] = slot_acc[pl.ds(d * nz, nz)].reshape(nz * HB, COLS).astype(BF16)
        start = pl.multiple_of(d * chunk, 16)
        out[d, nz * HB :, :] = rel_acc[pl.ds(start, chunk), :].astype(BF16)
        return carry

    lax.fori_loop(0, nx * ny, put, 0)


def backward(dims, chunk, meta, pos, rec_own, w_own, w_other, gagg_own, gagg_other, table, upd_sum):
    nx, nz, ny = dims
    slots, tiles = rec_own.shape[0], w_own.shape[0]
    places = 2 * (tiles // GROUP)
    return pl.pallas_call(
        functools.partial(backward_kernel, dims, tiles, chunk),
        out_shape=jax.ShapeDtypeStruct((nx * ny, nz * HB + chunk, COLS), BF16),
        in_specs=[SMEM_SPEC, SMEM_SPEC] + [ANY_SPEC] * 3 + [VMEM_SPEC] * 4,
        out_specs=VMEM_SPEC,
        scratch_shapes=[
            pltpu.VMEM((slots, HB, COLS), BF16),
            pltpu.VMEM((places, GROUP, HB, BLK), BF16),
            pltpu.VMEM((slots, HB, COLS), F32),
            pltpu.VMEM((nx * ny * chunk, COLS), F32),
            pltpu.VMEM((NB_DEV, BLK, COLS), BF16),
            pltpu.SemaphoreType.DMA((places,)),
            pltpu.SemaphoreType.DMA((1,)),
        ],
        compiler_params=params(),
        name="backward",
    )(meta, pos, rec_own, w_own, w_other, gagg_own, gagg_other, table, upd_sum)


def combine_kernel(dims, chunk, pos, sends, arrived, *refs):
    nx, nz, ny = dims
    outs, acc = refs[:nz], refs[nz]
    z = pos[1]
    nodes = nx * nz * ny
    acc[...] = jnp.zeros_like(acc)
    rel = jnp.zeros((chunk, COLS), F32)
    for s in range(nx * ny):
        sender = (s // ny) * (nz * ny) + z * ny + s % ny
        for owner in range(nz):
            k = lax.rem(z - owner + nz, nz)
            block = sends[k * nodes + sender]
            acc[owner, block] = acc[owner, block] + arrived[
                s, owner * HB : (owner + 1) * HB, :
            ].astype(F32)
        rel = rel + arrived[s, nz * HB :, :].astype(F32)
    for k in range(nz):
        owner = lax.rem(z + k, nz)
        outs[k][:ROWS, :] = acc[owner].reshape(ROWS, COLS).astype(outs[k].dtype)
        outs[k][ROWS:, :] = rel.astype(outs[k].dtype)


def combine(dims, chunk, pos, sends, arrived):
    nz = dims[1]
    shape = (ROWS + chunk, COLS)
    outs = (jax.ShapeDtypeStruct(shape, F32),) + (jax.ShapeDtypeStruct(shape, BF16),) * (nz - 1)
    return pl.pallas_call(
        functools.partial(combine_kernel, dims, chunk),
        out_shape=outs,
        in_specs=[SMEM_SPEC, SMEM_SPEC, VMEM_SPEC],
        out_specs=(VMEM_SPEC,) * nz,
        scratch_shapes=[pltpu.VMEM((nz, NB_DEV, HB, COLS), F32)],
        compiler_params=params(),
        name="combine",
    )(pos, sends, arrived)


def collect_kernel(count, more, *refs):
    parts, refs = refs[:count], refs[count:]
    total = parts[0][...]
    for part in parts[1:]:
        total = total + part[...].astype(F32)
    grad = refs[0][...].astype(F32) + total[:ROWS]
    if more:
        pre, aggregate, upd_t, block_mask, grad_ref, rel_ref, gagg_ref, upd_ref = refs[1:]
        before_backward(
            grad, pre[...], aggregate[...], upd_t[...], block_mask[...], gagg_ref, upd_ref
        )
    else:
        grad_ref, rel_ref = refs[1:]
    grad_ref[...] = grad
    rel_ref[...] = total[ROWS:]


def collect(chunk, parts, grad, more):
    outs = [jax.ShapeDtypeStruct((ROWS, COLS), F32), jax.ShapeDtypeStruct((chunk, COLS), F32)]
    if more:
        outs.append(jax.ShapeDtypeStruct((ROWS, COLS), BF16))
        outs.append(jax.ShapeDtypeStruct((H, COLS), F32))
    return pl.pallas_call(
        functools.partial(collect_kernel, len(parts), bool(more)),
        out_shape=tuple(outs),
        in_specs=[VMEM_SPEC] * (len(parts) + 1 + len(more)),
        out_specs=(VMEM_SPEC,) * len(outs),
        compiler_params=params(),
        name="collect_more" if more else "collect_last",
    )(*parts, grad, *more)


def place_kernel(dims, chunk, pos, *refs):
    nx, _, ny = dims
    out = refs[nx]
    for kx in range(nx):
        x = lax.rem(pos[0] - kx + nx, nx)
        for ky in range(ny):
            y = lax.rem(pos[2] - ky + ny, ny)
            start = pl.multiple_of((x * ny + y) * chunk, 16)
            out[pl.ds(start, chunk), :] = refs[kx][ky * chunk : (ky + 1) * chunk, :]


def shift(value, axis, count, k):
    return lax.ppermute(value, axis, [(s, (s + k) % count) for s in range(count)])


def gather_relations(dims, chunk, pos, rel):
    nx, _, ny = dims
    rel = rel + lax.ppermute(rel, "c", SWAP)
    along_y = jnp.concatenate([rel] + [shift(rel, "y", ny, k) for k in range(1, ny)])
    parts = [along_y] + [shift(along_y, "x", nx, k) for k in range(1, nx)]
    return pl.pallas_call(
        functools.partial(place_kernel, dims, chunk),
        out_shape=jax.ShapeDtypeStruct((nx * ny * chunk, COLS), F32),
        in_specs=[SMEM_SPEC] + [VMEM_SPEC] * nx,
        out_specs=VMEM_SPEC,
        compiler_params=params(),
        name="place",
    )(pos, *parts)


def whole_rows(core, own, other):
    own, other = (v.reshape(NB_DEV, 1, HB, COLS) for v in (own, other))
    low = jnp.where(core == 0, own, other)
    high = jnp.where(core == 0, other, own)
    return jnp.concatenate([low, high], axis=1).reshape(NB_DEV * BLK, COLS)


def body(dims, node_state, send_list, tile_weight, tile_slot, tile_dst, tile_rel, live_groups,
         query_rel, query_head, rel_table, rel_proj, upd_weight, cotangent):
    nx, nz, ny = dims
    nodes = nx * nz * ny
    chunk = -(-REL_ROWS // (nx * ny * 16)) * 16
    x, z, y, core = (lax.axis_index(a) for a in ("x", "z", "y", "c"))
    node = (x * nz + z) * ny + y
    pos = jnp.stack([x, z, y, core]).astype(jnp.int32)
    tiles = tile_weight.shape[2]

    def own_half(rows):
        return lax.dynamic_index_in_dim(
            rows.reshape(NB_DEV, 2, HB, COLS), core, 1, keepdims=False
        ).reshape(ROWS, COLS)

    def swap(value):
        return lax.ppermute(value, "c", SWAP)

    state = own_half(node_state)
    listed = jnp.pad(send_list.astype(BF16), ((0, 15), (0, COLS - nodes)))
    first = jnp.concatenate([state, listed])
    pieces = [first] + [shift(first, "z", nz, k) for k in range(1, nz)]
    sends = jnp.concatenate([p[ROWS : ROWS + 1, :nodes] for p in pieces])
    sends = sends.astype(jnp.int32).reshape(-1)

    slot = tile_slot[0, 0]
    slot = ((slot // (nz * ny)) * ny + slot % ny) * nz + (slot // ny) % nz
    live = jnp.broadcast_to(live_groups[0, 0], (tiles,))
    meta = jnp.stack([slot, tile_dst[0, 0], tile_rel[0, 0], live])
    meta = jnp.stack([meta, swap(meta)]).reshape(-1)

    f_own, f_send, b_own, b_send = split_weights(pos, tile_weight[0, 0])
    f_other, b_other = swap(f_send), swap(b_send)

    query_vec, tables = relation_vectors(rel_table, query_rel, rel_proj)
    row_ids = node * (NB_DEV * BLK) + (
        jnp.arange(NB_DEV, dtype=jnp.int32)[:, None] * BLK
        + core * HB
        + jnp.arange(HB, dtype=jnp.int32)[None, :]
    ).reshape(ROWS)
    matches = (row_ids[:, None] == query_head[None, :]).astype(F32)
    bound = (matches[:, :, None] * query_vec[None, :, :]).reshape(ROWS, COLS)
    lane_block = jnp.arange(COLS, dtype=jnp.int32) // H
    block_mask = (lane_block[:, None] == lane_block[None, :]).astype(F32)
    upd = [jnp.tile(upd_weight[l], (Q, Q)) * block_mask for l in range(L)]
    upd_t = [u.T for u in upd]
    cot = own_half(cotangent)

    received = []
    for l in range(L):
        if l:
            pieces = [state] + [shift(state, "z", nz, k) for k in range(1, nz)]
        outgoing = provide(dims, pos, sends, pieces)
        rec_own = lax.all_to_all(outgoing, ("x", "y"), 0, 0, tiled=True)
        rec_own = rec_own.reshape(nodes, HB, COLS)
        received.append(rec_own)
        last = l == L - 1
        more = (cot, upd_t[l], block_mask) if last else ()
        made = forward(
            last, meta, pos, rec_own, swap(rec_own), f_own, f_other, tables[l], bound, upd[l],
            state, more,
        )
        state = made[0]
        if last:
            gagg, upd_sum = made[1:]
        else:
            agg0, pre0 = made[1:]

    grad = cot
    relations = [None] * L
    for l in reversed(range(L)):
        sent = backward(
            dims, chunk, meta, pos, received[l], b_own, b_other, gagg, swap(gagg), tables[l],
            upd_sum,
        )
        arrived = lax.all_to_all(sent, ("x", "y"), 0, 0, tiled=True)
        parts = combine(dims, chunk, pos, sends, arrived)
        parts = [parts[0]] + [shift(parts[k], "z", nz, k) for k in range(1, nz)]
        more = (pre0, agg0, upd_t[0], block_mask) if l else ()
        made = collect(chunk, parts, grad, more)
        grad, rel = made[:2]
        if l:
            gagg, upd_sum = made[2:]
        relations[l] = gather_relations(dims, chunk, pos, rel)

    scale_factor = float(nodes * NB_DEV * BLK) ** (-0.5)
    projs = []
    upds = []
    for l in range(L):
        projs.append(
            jnp.einsum(
                "qh,rqk->hrk",
                query_vec,
                relations[l][:R].reshape(R, Q, H),
                precision=EXACT_MATMUL,
            ).reshape(H, R * H)
            * scale_factor
        )
        upds.append(relations[l][R8 : R8 + H].reshape(H, Q, H).sum(1))
    final_state = whole_rows(core, state, swap(state))
    grad_state = whole_rows(core, grad, swap(grad))
    return (
        final_state,
        grad_state,
        jnp.stack(projs).astype(BF16),
        jnp.stack(upds) * scale_factor,
    )


def solution(mesh):
    dims = grid_dims(mesh.shape["node"])
    fine = Mesh(mesh.devices.reshape(*dims, 2), ("x", "z", "y", "c"))
    node = ("x", "z", "y")
    return jax.shard_map(
        functools.partial(body, dims),
        mesh=fine,
        in_specs=(
            P(node, None),
            P(node, None),
            P(node, "c", None, None, None),
            P(node, "c", None),
            P(node, "c", None),
            P(node, "c", None),
            P(node, "c"),
            P(),
            P(),
            P(),
            P(),
            P(),
            P(node, None),
        ),
        out_specs=(P(node, None), P(node, None), P(), P()),
        check_vma=False,
    )
```

```python
import functools

import jax
import jax.numpy as jnp
from jax import lax
from jax.experimental import pallas as pl
from jax.experimental.pallas import tpu as pltpu
from jax.sharding import Mesh
from jax.sharding import PartitionSpec as P

H = 32
R = 535
BLK = 128
HB = BLK // 2
Q = 4
L = 2
GROUP = 16
NB_DEV = 4
COLS = Q * H
ROWS = NB_DEV * HB
R8 = 536
REL_ROWS = R8 + H
F32 = jnp.float32
BF16 = jnp.bfloat16
EXACT_MATMUL = lax.Precision.HIGHEST
VMEM_LIMIT = 48 * 1024 * 1024
SWAP = [(0, 1), (1, 0)]
SMEM_SPEC = pl.BlockSpec(memory_space=pltpu.SMEM)
VMEM_SPEC = pl.BlockSpec(memory_space=pltpu.VMEM)
ANY_SPEC = pl.BlockSpec(memory_space=pl.ANY)


def grid_dims(node_count):
    if node_count == 128:
        return (4, 8, 4)
    return (2, node_count // 4, 2)


def params():
    return pltpu.CompilerParams(vmem_limit_bytes=VMEM_LIMIT)


def query_vectors(rel_table, query_rel):
    relation_ids = jnp.arange(R, dtype=jnp.int32)
    picked = (query_rel[:, None] == relation_ids[None, :]).astype(F32)
    return jnp.dot(picked, rel_table, precision=EXACT_MATMUL)


def relation_table(query_vec, proj):
    flat_rows = jnp.dot(query_vec, proj.astype(F32), precision=EXACT_MATMUL)
    table = flat_rows.reshape(Q, R, H).transpose(1, 0, 2).reshape(R, COLS)
    return jnp.pad(table, ((0, R8 - R), (0, 0)))


def split_kernel(pos, w_ref, f_keep, f_send, b_keep, b_send):
    core = pos[3]
    own = pl.multiple_of(core * HB, HB)
    other = pl.multiple_of((1 - core) * HB, HB)
    f_keep[...] = w_ref[:, pl.ds(own, HB), :]
    f_send[...] = w_ref[:, pl.ds(other, HB), :]
    for t in range(w_ref.shape[0]):
        flipped = w_ref[t].T
        low, high = flipped[:HB], flipped[HB:]
        b_keep[t] = jnp.where(core == 0, low, high)
        b_send[t] = jnp.where(core == 0, high, low)


def split_weights(pos, weights):
    tiles = weights.shape[0]
    half = jax.ShapeDtypeStruct((tiles, HB, BLK), BF16)
    spec = pl.BlockSpec((GROUP, HB, BLK), lambda g: (g, 0, 0))
    return pl.pallas_call(
        split_kernel,
        out_shape=(half,) * 4,
        grid=(tiles // GROUP,),
        in_specs=[SMEM_SPEC, pl.BlockSpec((GROUP, BLK, BLK), lambda g: (g, 0, 0))],
        out_specs=[spec] * 4,
        compiler_params=params(),
        cost_estimate=pl.CostEstimate(
            flops=0, bytes_accessed=tiles * BLK * BLK * 2 * 3, transcendentals=0
        ),
        name="split_weights",
    )(pos, weights)


def provide_kernel(dims, pos, sends, column, out):
    nx, nz, ny = dims
    z = pos[1]
    nodes = nx * nz * ny
    for owner in range(nz):
        for d in range(nx * ny):
            reader = (d // ny) * (nz * ny) + z * ny + d % ny
            block = sends[owner * nodes + reader]
            start = pl.multiple_of(block * HB, HB)
            out[d, owner] = column[owner, pl.ds(start, HB), :]


def provide(dims, pos, sends, column):
    nx, nz, ny = dims
    return pl.pallas_call(
        functools.partial(provide_kernel, dims),
        out_shape=jax.ShapeDtypeStruct((nx * ny, nz, HB, COLS), BF16),
        in_specs=[SMEM_SPEC, SMEM_SPEC, VMEM_SPEC],
        out_specs=VMEM_SPEC,
        compiler_params=params(),
        name="provide",
    )(pos, sends, column)


def start_weights(meta, tiles, weights, buffer, sems):
    groups = tiles // GROUP
    for source in range(2):
        live = meta[(source * 4 + 3) * tiles]
        for g in range(groups):

            @pl.when(g < live)
            def _(source=source, g=g):
                pltpu.make_async_copy(
                    weights[source].at[pl.ds(g * GROUP, GROUP)],
                    buffer.at[source * groups + g],
                    sems.at[source * groups + g],
                ).start()


def over_tiles(meta, tiles, weights, buffer, sems, one_tile):
    groups = tiles // GROUP
    for source in range(2):
        live = meta[(source * 4 + 3) * tiles]
        base = source * 4 * tiles

        def one_group(g, carry, source=source, base=base):
            place = source * groups + g
            pltpu.make_async_copy(
                weights[source].at[pl.ds(g * GROUP, GROUP)],
                buffer.at[place],
                sems.at[place],
            ).wait()
            for t in range(GROUP):
                at = base + g * GROUP + t
                one_tile(
                    buffer[place, t],
                    meta[at],
                    meta[at + tiles],
                    meta[at + 2 * tiles],
                )
            return carry

        lax.fori_loop(0, live, one_group, 0)


def update_terms(aggregate, grad_pre, block_mask):
    product = jnp.dot(aggregate.T, grad_pre, precision=EXACT_MATMUL, preferred_element_type=F32)
    product = product * block_mask
    total = product[:H]
    for q in range(1, Q):
        total = total + product[q * H : (q + 1) * H]
    return total


def before_backward(grad, pre, aggregate, upd_t, block_mask, gagg_ref, upd_ref):
    sigma = jax.nn.sigmoid(pre)
    grad_pre = grad * (sigma * (1.0 + pre * (1.0 - sigma)))
    gagg_ref[...] = jnp.dot(
        grad_pre, upd_t, precision=EXACT_MATMUL, preferred_element_type=F32
    ).astype(BF16)
    upd_ref[...] = update_terms(aggregate, grad_pre, block_mask)


def forward_kernel(last, tiles, meta, pos, rec_own, rec_other, w_own, w_other, table, bound,
                   upd, state, *refs):
    if last:
        cotangent, upd_t, block_mask = refs[:3]
        next_ref, gagg_ref, upd_ref, rec, buffer, acc, w_sems, r_sems = refs[3:]
    else:
        next_ref, agg_ref, pre_ref, rec, buffer, acc, w_sems, r_sems = refs
    own = pl.multiple_of(pos[3] * HB, HB)
    other = pl.multiple_of((1 - pos[3]) * HB, HB)
    copies = [
        pltpu.make_async_copy(rec_own, rec.at[:, pl.ds(own, HB), :], r_sems.at[0]),
        pltpu.make_async_copy(rec_other, rec.at[:, pl.ds(other, HB), :], r_sems.at[1]),
    ]
    for copy in copies:
        copy.start()
    start_weights(meta, tiles, (w_own, w_other), buffer, w_sems)
    acc[...] = jnp.zeros_like(acc)
    for copy in copies:
        copy.wait()

    def one_tile(weight, slot, dst, rel):
        message = jnp.dot(weight, rec[slot], preferred_element_type=F32)
        acc[dst] = acc[dst] + message * table[pl.ds(rel, 1), :]

    over_tiles(meta, tiles, (w_own, w_other), buffer, w_sems, one_tile)
    aggregate = acc[...].reshape(ROWS, COLS) + bound[...]
    pre = jnp.dot(aggregate, upd[...], precision=EXACT_MATMUL, preferred_element_type=F32)
    next_ref[...] = (state[...].astype(F32) + pre * jax.nn.sigmoid(pre)).astype(BF16)
    if last:
        before_backward(
            cotangent[...].astype(F32), pre, aggregate, upd_t[...], block_mask[...],
            gagg_ref, upd_ref,
        )
    else:
        agg_ref[...] = aggregate
        pre_ref[...] = pre


def forward(last, meta, pos, rec_own, rec_other, w_own, w_other, table, bound, upd, state, more):
    slots, tiles = rec_own.shape[0], w_own.shape[0]
    places = 2 * (tiles // GROUP)
    rows16 = jax.ShapeDtypeStruct((ROWS, COLS), BF16)
    rows32 = jax.ShapeDtypeStruct((ROWS, COLS), F32)
    if last:
        outs = (rows16, rows16, jax.ShapeDtypeStruct((H, COLS), F32))
    else:
        outs = (rows16, rows32, rows32)
    return pl.pallas_call(
        functools.partial(forward_kernel, last, tiles),
        out_shape=outs,
        in_specs=[SMEM_SPEC, SMEM_SPEC] + [ANY_SPEC] * 4 + [VMEM_SPEC] * (4 + len(more)),
        out_specs=(VMEM_SPEC,) * 3,
        scratch_shapes=[
            pltpu.VMEM((slots, BLK, COLS), BF16),
            pltpu.VMEM((places, GROUP, HB, BLK), BF16),
            pltpu.VMEM((NB_DEV, HB, COLS), F32),
            pltpu.SemaphoreType.DMA((places,)),
            pltpu.SemaphoreType.DMA((2,)),
        ],
        compiler_params=params(),
        name="forward_last" if last else "forward_first",
    )(meta, pos, rec_own, rec_other, w_own, w_other, table, bound, upd, state, *more)


def backward_kernel(dims, tiles, chunk, meta, pos, rec_own, w_own, w_other, gagg_own,
                    gagg_other, table, upd_sum, *refs):
    passed, refs = refs[:-8], refs[-8:]
    out, rec, buffer, slot_acc, rel_acc, gagg, w_sems, r_sem = refs
    nx, nz, ny = dims
    copy = pltpu.make_async_copy(rec_own, rec, r_sem.at[0])
    copy.start()
    start_weights(meta, tiles, (w_own, w_other), buffer, w_sems)
    own = pl.multiple_of(pos[3] * HB, HB)
    other = pl.multiple_of((1 - pos[3]) * HB, HB)
    gagg[:, pl.ds(own, HB), :] = gagg_own[...].reshape(NB_DEV, HB, COLS)
    gagg[:, pl.ds(other, HB), :] = gagg_other[...].reshape(NB_DEV, HB, COLS)
    rel_acc[...] = jnp.zeros_like(rel_acc)
    rel_acc[R8 : R8 + H, :] = upd_sum[...]

    def clear(d, carry):
        slot_acc[pl.ds(d * nz, nz)] = jnp.zeros((nz, HB, COLS), F32)
        return carry

    lax.fori_loop(0, nx * ny, clear, 0)
    copy.wait()

    def one_tile(weight, slot, dst, rel):
        back = jnp.dot(weight, gagg[dst], preferred_element_type=F32)
        row = pl.ds(rel, 1)
        slot_acc[slot] = slot_acc[slot] + back * table[row, :]
        terms = jnp.sum(back * rec[slot].astype(F32), axis=0, keepdims=True)
        rel_acc[row, :] = rel_acc[row, :] + terms

    over_tiles(meta, tiles, (w_own, w_other), buffer, w_sems, one_tile)

    def put(d, carry):
        out[d, : nz * HB, :] = slot_acc[pl.ds(d * nz, nz)].reshape(nz * HB, COLS).astype(BF16)
        start = pl.multiple_of(d * chunk, 16)
        out[d, nz * HB : nz * HB + chunk, :] = rel_acc[pl.ds(start, chunk), :].astype(BF16)
        for part in passed:
            out[d, nz * HB + chunk :, :] = part[...].astype(BF16)
        return carry

    lax.fori_loop(0, nx * ny, put, 0)


def backward(dims, chunk, meta, pos, rec_own, w_own, w_other, gagg_own, gagg_other, table, upd_sum,
             passed):
    nx, nz, ny = dims
    slots, tiles = rec_own.shape[0], w_own.shape[0]
    places = 2 * (tiles // GROUP)
    return pl.pallas_call(
        functools.partial(backward_kernel, dims, tiles, chunk),
        out_shape=jax.ShapeDtypeStruct(
            (nx * ny, nz * HB + chunk * (1 + len(passed)), COLS), BF16
        ),
        in_specs=[SMEM_SPEC, SMEM_SPEC] + [ANY_SPEC] * 3 + [VMEM_SPEC] * (4 + len(passed)),
        out_specs=VMEM_SPEC,
        scratch_shapes=[
            pltpu.VMEM((slots, HB, COLS), BF16),
            pltpu.VMEM((places, GROUP, HB, BLK), BF16),
            pltpu.VMEM((slots, HB, COLS), F32),
            pltpu.VMEM((nx * ny * chunk, COLS), F32),
            pltpu.VMEM((NB_DEV, BLK, COLS), BF16),
            pltpu.SemaphoreType.DMA((places,)),
            pltpu.SemaphoreType.DMA((1,)),
        ],
        compiler_params=params(),
        name="backward",
    )(meta, pos, rec_own, w_own, w_other, gagg_own, gagg_other, table, upd_sum, *passed)


def combine_kernel(dims, chunk, pos, sends, arrived, out, *refs):
    acc = refs[-1]
    nx, nz, ny = dims
    z = pos[1]
    nodes = nx * nz * ny
    acc[...] = jnp.zeros_like(acc)
    rel = jnp.zeros((chunk, COLS), F32)
    for s in range(nx * ny):
        sender = (s // ny) * (nz * ny) + z * ny + s % ny
        for owner in range(nz):
            block = sends[owner * nodes + sender]
            acc[owner, block] = acc[owner, block] + arrived[
                s, owner * HB : (owner + 1) * HB, :
            ].astype(F32)
        rel = rel + arrived[s, nz * HB : nz * HB + chunk, :].astype(F32)
        for whole in refs[:-1]:
            whole[s * chunk : (s + 1) * chunk, :] = arrived[s, nz * HB + chunk :, :].astype(F32)
    for owner in range(nz):
        out[owner, :ROWS, :] = acc[owner].reshape(ROWS, COLS).astype(BF16)
        out[owner, ROWS:, :] = rel.astype(BF16)


def combine(dims, chunk, pos, sends, arrived):
    nx, nz, ny = dims
    outs = [jax.ShapeDtypeStruct((nz, ROWS + chunk, COLS), BF16)]
    if arrived.shape[1] > nz * HB + chunk:
        outs.append(jax.ShapeDtypeStruct((nx * ny * chunk, COLS), F32))
    return pl.pallas_call(
        functools.partial(combine_kernel, dims, chunk),
        out_shape=outs,
        in_specs=[SMEM_SPEC, SMEM_SPEC, VMEM_SPEC],
        out_specs=[VMEM_SPEC] * len(outs),
        scratch_shapes=[pltpu.VMEM((nz, NB_DEV, HB, COLS), F32)],
        compiler_params=params(),
        name="combine",
    )(pos, sends, arrived)


def collect_kernel(more, parts, *refs):
    total = parts[0].astype(F32)
    for k in range(1, parts.shape[0]):
        total = total + parts[k].astype(F32)
    grad = refs[0][...].astype(F32) + total[:ROWS]
    if more:
        pre, aggregate, upd_t, block_mask, grad_ref, rel_ref, gagg_ref, upd_ref = refs[1:]
        before_backward(
            grad, pre[...], aggregate[...], upd_t[...], block_mask[...], gagg_ref, upd_ref
        )
    else:
        grad_ref, rel_ref = refs[1:]
    grad_ref[...] = grad
    rel_ref[...] = total[ROWS:]


def collect(chunk, parts, grad, more):
    outs = [jax.ShapeDtypeStruct((ROWS, COLS), F32), jax.ShapeDtypeStruct((chunk, COLS), F32)]
    if more:
        outs.append(jax.ShapeDtypeStruct((ROWS, COLS), BF16))
        outs.append(jax.ShapeDtypeStruct((H, COLS), F32))
    return pl.pallas_call(
        functools.partial(collect_kernel, bool(more)),
        out_shape=tuple(outs),
        in_specs=[VMEM_SPEC] * (2 + len(more)),
        out_specs=(VMEM_SPEC,) * len(outs),
        compiler_params=params(),
        name="collect_more" if more else "collect_last",
    )(parts, grad, *more)


def gather_relations(dims, rel):
    count = dims[0] * dims[2]
    copies = jnp.broadcast_to(rel[None], (count,) + rel.shape)
    parts = lax.all_to_all(copies, ("x", "y"), 0, 0, tiled=True)
    return parts.reshape(count * rel.shape[0], COLS)


def whole_rows(core, own, other):
    own, other = (v.reshape(NB_DEV, 1, HB, COLS) for v in (own, other))
    low = jnp.where(core == 0, own, other)
    high = jnp.where(core == 0, other, own)
    return jnp.concatenate([low, high], axis=1).reshape(NB_DEV * BLK, COLS)


def body(dims, node_state, send_list, tile_weight, tile_slot, tile_dst, tile_rel, live_groups,
         query_rel, query_head, rel_table, rel_proj, upd_weight, cotangent):
    nx, nz, ny = dims
    nodes = nx * nz * ny
    chunk = -(-REL_ROWS // (nx * ny * 16)) * 16
    x, z, y, core = (lax.axis_index(a) for a in ("x", "z", "y", "c"))
    node = (x * nz + z) * ny + y
    pos = jnp.stack([x, z, y, core]).astype(jnp.int32)
    tiles = tile_weight.shape[2]

    def own_half(rows):
        return lax.dynamic_index_in_dim(
            rows.reshape(NB_DEV, 2, HB, COLS), core, 1, keepdims=False
        ).reshape(ROWS, COLS)

    def swap(value):
        return lax.ppermute(value, "c", SWAP)

    def column_of(rows):
        copies = jnp.broadcast_to(rows[None], (nz,) + rows.shape)
        return lax.all_to_all(copies, "z", 0, 0, tiled=True)

    state = own_half(node_state)
    listed = jnp.pad(send_list.astype(BF16), ((0, 15), (0, COLS - nodes)))
    column = column_of(jnp.concatenate([state, listed]))

    slot = tile_slot[0, 0]
    slot = ((slot // (nz * ny)) * ny + slot % ny) * nz + (slot // ny) % nz
    live = jnp.broadcast_to(live_groups[0, 0], (tiles,))
    meta = jnp.stack([slot, tile_dst[0, 0], tile_rel[0, 0], live])
    meta = jnp.stack([meta, swap(meta)]).reshape(-1)

    lane_block = jnp.arange(COLS, dtype=jnp.int32) // H
    block_mask = (lane_block[:, None] == lane_block[None, :]).astype(F32)
    upd = [jnp.tile(upd_weight[l], (Q, Q)) * block_mask for l in range(L)]
    upd_t = [u.T for u in upd]
    cot = own_half(cotangent)
    column, meta, upd, upd_t, block_mask, cot = lax.optimization_barrier(
        (column, meta, upd, upd_t, block_mask, cot)
    )
    sends = column[:, ROWS, :nodes].astype(jnp.int32).reshape(-1)
    outgoing = provide(dims, pos, sends, column)
    outgoing, later, query_rel = lax.optimization_barrier((outgoing, pos, query_rel))
    f_own, f_send, b_own, b_send = split_weights(later, tile_weight[0, 0])
    f_other, b_other = swap(f_send), swap(b_send)
    query_vec = query_vectors(rel_table, query_rel)
    row_ids = node * (NB_DEV * BLK) + (
        jnp.arange(NB_DEV, dtype=jnp.int32)[:, None] * BLK
        + core * HB
        + jnp.arange(HB, dtype=jnp.int32)[None, :]
    ).reshape(ROWS)
    matches = (row_ids[:, None] == query_head[None, :]).astype(F32)
    bound = (matches[:, :, None] * query_vec[None, :, :]).reshape(ROWS, COLS)

    received, tables = [], []
    for l in range(L):
        if l:
            outgoing = provide(dims, pos, sends, column_of(state))
            outgoing, vectors = lax.optimization_barrier((outgoing, query_vec))
        else:
            vectors = query_vec
        rec_own = lax.all_to_all(outgoing, ("x", "y"), 0, 0, tiled=True)
        table = relation_table(vectors, rel_proj[l])
        if l:
            rec_own, table = lax.optimization_barrier((rec_own, table))
        else:
            rec_own, table, bound, f_own, f_other, b_own, b_other = lax.optimization_barrier(
                (rec_own, table, bound, f_own, f_other, b_own, b_other)
            )
        tables.append(table)
        rec_own = rec_own.reshape(nodes, HB, COLS)
        received.append(rec_own)
        last = l == L - 1
        more = (cot, upd_t[l], block_mask) if last else ()
        made = forward(
            last, meta, pos, rec_own, swap(rec_own), f_own, f_other, tables[l], bound, upd[l],
            state, more,
        )
        state = made[0]
        if last:
            gagg, upd_sum = made[1:]
        else:
            agg0, pre0 = made[1:]

    grad = cot
    passed = ()
    relations = [None] * L
    for l in reversed(range(L)):
        sent = backward(
            dims, chunk, meta, pos, received[l], b_own, b_other, gagg, swap(gagg), tables[l],
            upd_sum, passed,
        )
        arrived = lax.all_to_all(sent, ("x", "y"), 0, 0, tiled=True)
        combined, *whole = combine(dims, chunk, pos, sends, arrived)
        parts = lax.all_to_all(combined, "z", 0, 0, tiled=True)
        more = (pre0, agg0, upd_t[0], block_mask) if l else ()
        made = collect(chunk, parts, grad, more)
        grad, rel = made[:2]
        if l:
            gagg, upd_sum = made[2:]
        rel = rel + swap(rel)
        passed = (rel,) if l else ()
        if whole:
            relations[l + 1] = whole[0]
    relations[0] = gather_relations(dims, rel)

    scale_factor = float(nodes * NB_DEV * BLK) ** (-0.5)
    projs = []
    upds = []
    for l in range(L):
        projs.append(
            jnp.einsum(
                "qh,rqk->hrk",
                query_vec,
                relations[l][:R].reshape(R, Q, H),
                precision=EXACT_MATMUL,
            ).reshape(H, R * H)
            * scale_factor
        )
        upds.append(relations[l][R8 : R8 + H].reshape(H, Q, H).sum(1))
    final_state = whole_rows(core, state, swap(state))
    grad_state = whole_rows(core, grad, swap(grad))
    return (
        final_state,
        grad_state,
        jnp.stack(projs).astype(BF16),
        jnp.stack(upds) * scale_factor,
    )


def solution(mesh):
    dims = grid_dims(mesh.shape["node"])
    fine = Mesh(mesh.devices.reshape(*dims, 2), ("x", "z", "y", "c"))
    node = ("x", "z", "y")
    return jax.shard_map(
        functools.partial(body, dims),
        mesh=fine,
        in_specs=(
            P(node, None),
            P(node, None),
            P(node, "c", None, None, None),
            P(node, "c", None),
            P(node, "c", None),
            P(node, "c", None),
            P(node, "c"),
            P(),
            P(),
            P(),
            P(),
            P(),
            P(node, None),
        ),
        out_specs=(P(node, None), P(node, None), P(), P()),
        check_vma=False,
    )
```

```python
import functools

import jax
import jax.numpy as jnp
from jax import lax
from jax.experimental import pallas as pl
from jax.experimental.pallas import tpu as pltpu
from jax.sharding import Mesh
from jax.sharding import PartitionSpec as P

H = 32
R = 535
BLK = 128
HB = BLK // 2
Q = 4
L = 2
GROUP = 16
NB_DEV = 4
COLS = Q * H
ROWS = NB_DEV * HB
R8 = 536
REL_ROWS = R8 + H
F32 = jnp.float32
BF16 = jnp.bfloat16
EXACT_MATMUL = lax.Precision.HIGHEST
VMEM_LIMIT = 48 * 1024 * 1024
SWAP = [(0, 1), (1, 0)]
SMEM_SPEC = pl.BlockSpec(memory_space=pltpu.SMEM)
VMEM_SPEC = pl.BlockSpec(memory_space=pltpu.VMEM)
ANY_SPEC = pl.BlockSpec(memory_space=pl.ANY)


def grid_dims(node_count):
    if node_count == 128:
        return (4, 8, 4)
    return (2, node_count // 4, 2)


def params():
    return pltpu.CompilerParams(vmem_limit_bytes=VMEM_LIMIT)


def query_vectors(rel_table, query_rel):
    relation_ids = jnp.arange(R, dtype=jnp.int32)
    picked = (query_rel[:, None] == relation_ids[None, :]).astype(F32)
    return jnp.dot(picked, rel_table, precision=EXACT_MATMUL)


def relation_table(query_vec, proj):
    flat_rows = jnp.dot(query_vec, proj.astype(F32), precision=EXACT_MATMUL)
    table = flat_rows.reshape(Q, R, H).transpose(1, 0, 2).reshape(R, COLS)
    return jnp.pad(table, ((0, R8 - R), (0, 0)))


def split_kernel(pos, w_ref, keep, send):
    core = pos[3]
    for t in range(w_ref.shape[0]):
        flipped = w_ref[t].T
        low, high = flipped[:HB], flipped[HB:]
        keep[t] = jnp.where(core == 0, low, high)
        send[t] = jnp.where(core == 0, high, low)


def split_weights(pos, weights):
    tiles = weights.shape[0]
    half = jax.ShapeDtypeStruct((tiles, HB, BLK), BF16)
    spec = pl.BlockSpec((GROUP, HB, BLK), lambda g: (g, 0, 0))
    return pl.pallas_call(
        split_kernel,
        out_shape=(half,) * 2,
        grid=(tiles // GROUP,),
        in_specs=[SMEM_SPEC, pl.BlockSpec((GROUP, BLK, BLK), lambda g: (g, 0, 0))],
        out_specs=[spec] * 2,
        compiler_params=params(),
        cost_estimate=pl.CostEstimate(
            flops=0, bytes_accessed=tiles * BLK * BLK * 2 * 2, transcendentals=0
        ),
        name="split_weights",
    )(pos, weights)


def provide_kernel(dims, pos, sends, column, out):
    nx, nz, ny = dims
    z = pos[1]
    nodes = nx * nz * ny
    for owner in range(nz):
        for d in range(nx * ny):
            reader = (d // ny) * (nz * ny) + z * ny + d % ny
            block = sends[owner * nodes + reader]
            start = pl.multiple_of(block * HB, HB)
            out[d, owner] = column[owner, pl.ds(start, HB), :]


def provide(dims, pos, sends, column):
    nx, nz, ny = dims
    return pl.pallas_call(
        functools.partial(provide_kernel, dims),
        out_shape=jax.ShapeDtypeStruct((nx * ny, nz, HB, COLS), BF16),
        in_specs=[SMEM_SPEC, SMEM_SPEC, VMEM_SPEC],
        out_specs=VMEM_SPEC,
        compiler_params=params(),
        name="provide",
    )(pos, sends, column)


def start_weights(meta, tiles, weights, buffer, sems):
    groups = tiles // GROUP
    for source in range(2):
        live = meta[(source * 4 + 3) * tiles]
        for g in range(groups):

            @pl.when(g < live)
            def _(source=source, g=g):
                pltpu.make_async_copy(
                    weights[source](pl.ds(g * GROUP, GROUP)),
                    buffer.at[source * groups + g],
                    sems.at[source * groups + g],
                ).start()


def over_tiles(meta, tiles, weights, buffer, sems, one_tile):
    groups = tiles // GROUP
    for source in range(2):
        live = meta[(source * 4 + 3) * tiles]
        base = source * 4 * tiles

        def one_group(g, carry, source=source, base=base):
            place = source * groups + g
            pltpu.make_async_copy(
                weights[source](pl.ds(g * GROUP, GROUP)),
                buffer.at[place],
                sems.at[place],
            ).wait()
            for t in range(GROUP):
                at = base + g * GROUP + t
                one_tile(
                    buffer[place, t],
                    meta[at],
                    meta[at + tiles],
                    meta[at + 2 * tiles],
                )
            return carry

        lax.fori_loop(0, live, one_group, 0)


def update_terms(aggregate, grad_pre, block_mask):
    product = jnp.dot(aggregate.T, grad_pre, precision=EXACT_MATMUL, preferred_element_type=F32)
    product = product * block_mask
    total = product[:H]
    for q in range(1, Q):
        total = total + product[q * H : (q + 1) * H]
    return total


def before_backward(grad, pre, aggregate, upd_t, block_mask, gagg_ref, upd_ref):
    sigma = jax.nn.sigmoid(pre)
    grad_pre = grad * (sigma * (1.0 + pre * (1.0 - sigma)))
    gagg_ref[...] = jnp.dot(
        grad_pre, upd_t, precision=EXACT_MATMUL, preferred_element_type=F32
    ).astype(BF16)
    upd_ref[...] = update_terms(aggregate, grad_pre, block_mask)


def forward_kernel(last, tiles, meta, pos, rec_own, rec_other, w_own, w_other, table, bound,
                   upd, state, *refs):
    if last:
        cotangent, upd_t, block_mask = refs[:3]
        next_ref, gagg_ref, upd_ref, rec, buffer, acc, w_sems, r_sems = refs[3:]
    else:
        next_ref, agg_ref, pre_ref, rec, buffer, acc, w_sems, r_sems = refs
    own = pl.multiple_of(pos[3] * HB, HB)
    other = pl.multiple_of((1 - pos[3]) * HB, HB)
    copies = [
        pltpu.make_async_copy(rec_own, rec.at[:, pl.ds(own, HB), :], r_sems.at[0]),
        pltpu.make_async_copy(rec_other, rec.at[:, pl.ds(other, HB), :], r_sems.at[1]),
    ]
    for copy in copies:
        copy.start()
    weights = (lambda g: w_own.at[g, pl.ds(own, HB), :], lambda g: w_other.at[g])
    start_weights(meta, tiles, weights, buffer, w_sems)
    acc[...] = jnp.zeros_like(acc)
    for copy in copies:
        copy.wait()

    def one_tile(weight, slot, dst, rel):
        message = jnp.dot(weight, rec[slot], preferred_element_type=F32)
        acc[dst] = acc[dst] + message * table[pl.ds(rel, 1), :]

    over_tiles(meta, tiles, weights, buffer, w_sems, one_tile)
    aggregate = acc[...].reshape(ROWS, COLS) + bound[...]
    pre = jnp.dot(aggregate, upd[...], precision=EXACT_MATMUL, preferred_element_type=F32)
    next_ref[...] = (state[...].astype(F32) + pre * jax.nn.sigmoid(pre)).astype(BF16)
    if last:
        before_backward(
            cotangent[...].astype(F32), pre, aggregate, upd_t[...], block_mask[...],
            gagg_ref, upd_ref,
        )
    else:
        agg_ref[...] = aggregate
        pre_ref[...] = pre


def forward(last, meta, pos, rec_own, rec_other, w_own, w_other, table, bound, upd, state, more):
    slots, tiles = rec_own.shape[0], w_own.shape[0]
    places = 2 * (tiles // GROUP)
    rows16 = jax.ShapeDtypeStruct((ROWS, COLS), BF16)
    rows32 = jax.ShapeDtypeStruct((ROWS, COLS), F32)
    if last:
        outs = (rows16, rows16, jax.ShapeDtypeStruct((H, COLS), F32))
    else:
        outs = (rows16, rows32, rows32)
    return pl.pallas_call(
        functools.partial(forward_kernel, last, tiles),
        out_shape=outs,
        in_specs=[SMEM_SPEC, SMEM_SPEC] + [ANY_SPEC] * 4 + [VMEM_SPEC] * (4 + len(more)),
        out_specs=(VMEM_SPEC,) * 3,
        scratch_shapes=[
            pltpu.VMEM((slots, BLK, COLS), BF16),
            pltpu.VMEM((places, GROUP, HB, BLK), BF16),
            pltpu.VMEM((NB_DEV, HB, COLS), F32),
            pltpu.SemaphoreType.DMA((places,)),
            pltpu.SemaphoreType.DMA((2,)),
        ],
        compiler_params=params(),
        name="forward_last" if last else "forward_first",
    )(meta, pos, rec_own, rec_other, w_own, w_other, table, bound, upd, state, *more)


def backward_kernel(dims, tiles, meta, pos, rec_own, w_own, w_other, gagg_own,
                    gagg_other, table, upd_sum, out, rel_acc, rec, buffer, slot_acc, gagg,
                    w_sems, r_sem):
    nx, nz, ny = dims
    copy = pltpu.make_async_copy(rec_own, rec, r_sem.at[0])
    copy.start()
    weights = (lambda g: w_own.at[g], lambda g: w_other.at[g])
    start_weights(meta, tiles, weights, buffer, w_sems)
    own = pl.multiple_of(pos[3] * HB, HB)
    other = pl.multiple_of((1 - pos[3]) * HB, HB)
    gagg[:, pl.ds(own, HB), :] = gagg_own[...].reshape(NB_DEV, HB, COLS)
    gagg[:, pl.ds(other, HB), :] = gagg_other[...].reshape(NB_DEV, HB, COLS)
    rel_acc[...] = jnp.zeros_like(rel_acc)
    rel_acc[R8 : R8 + H, :] = upd_sum[...]

    def clear(d, carry):
        slot_acc[pl.ds(d * nz, nz)] = jnp.zeros((nz, HB, COLS), F32)
        return carry

    lax.fori_loop(0, nx * ny, clear, 0)
    copy.wait()

    def one_tile(weight, slot, dst, rel):
        back = jnp.dot(weight, gagg[dst], preferred_element_type=F32)
        row = pl.ds(rel, 1)
        slot_acc[slot] = slot_acc[slot] + back * table[row, :]
        terms = jnp.sum(back * rec[slot].astype(F32), axis=0, keepdims=True)
        rel_acc[row, :] = rel_acc[row, :] + terms

    over_tiles(meta, tiles, weights, buffer, w_sems, one_tile)

    def put(d, carry):
        out[d] = slot_acc[pl.ds(d * nz, nz)].reshape(nz * HB, COLS).astype(BF16)
        return carry

    lax.fori_loop(0, nx * ny, put, 0)


def backward(dims, rel_rows, meta, pos, rec_own, w_own, w_other, gagg_own, gagg_other, table,
             upd_sum):
    nx, nz, ny = dims
    slots, tiles = rec_own.shape[0], w_own.shape[0]
    places = 2 * (tiles // GROUP)
    return pl.pallas_call(
        functools.partial(backward_kernel, dims, tiles),
        out_shape=(
            jax.ShapeDtypeStruct((nx * ny, nz * HB, COLS), BF16),
            jax.ShapeDtypeStruct((rel_rows, COLS), F32),
        ),
        in_specs=[SMEM_SPEC, SMEM_SPEC] + [ANY_SPEC] * 3 + [VMEM_SPEC] * 4,
        out_specs=(VMEM_SPEC, VMEM_SPEC),
        scratch_shapes=[
            pltpu.VMEM((slots, HB, COLS), BF16),
            pltpu.VMEM((places, GROUP, HB, BLK), BF16),
            pltpu.VMEM((slots, HB, COLS), F32),
            pltpu.VMEM((NB_DEV, BLK, COLS), BF16),
            pltpu.SemaphoreType.DMA((places,)),
            pltpu.SemaphoreType.DMA((1,)),
        ],
        compiler_params=params(),
        name="backward",
    )(meta, pos, rec_own, w_own, w_other, gagg_own, gagg_other, table, upd_sum)


def combine_kernel(dims, pos, sends, arrived, out, acc):
    nx, nz, ny = dims
    z = pos[1]
    nodes = nx * nz * ny
    acc[...] = jnp.zeros_like(acc)
    for s in range(nx * ny):
        sender = (s // ny) * (nz * ny) + z * ny + s % ny
        for owner in range(nz):
            block = sends[owner * nodes + sender]
            acc[owner, block] = acc[owner, block] + arrived[
                s, owner * HB : (owner + 1) * HB, :
            ].astype(F32)
    for owner in range(nz):
        out[owner] = acc[owner].reshape(ROWS, COLS).astype(BF16)


def combine(dims, pos, sends, arrived):
    nz = dims[1]
    return pl.pallas_call(
        functools.partial(combine_kernel, dims),
        out_shape=jax.ShapeDtypeStruct((nz, ROWS, COLS), BF16),
        in_specs=[SMEM_SPEC, SMEM_SPEC, VMEM_SPEC],
        out_specs=VMEM_SPEC,
        scratch_shapes=[pltpu.VMEM((nz, NB_DEV, HB, COLS), F32)],
        compiler_params=params(),
        name="combine",
    )(pos, sends, arrived)


def collect_kernel(more, parts, *refs):
    total = parts[0].astype(F32)
    for k in range(1, parts.shape[0]):
        total = total + parts[k].astype(F32)
    grad = refs[0][...].astype(F32) + total
    if more:
        pre, aggregate, upd_t, block_mask, grad_ref, gagg_ref, upd_ref = refs[1:]
        before_backward(
            grad, pre[...], aggregate[...], upd_t[...], block_mask[...], gagg_ref, upd_ref
        )
    else:
        grad_ref = refs[1]
    grad_ref[...] = grad


def collect(parts, grad, more):
    outs = [jax.ShapeDtypeStruct((ROWS, COLS), F32)]
    if more:
        outs.append(jax.ShapeDtypeStruct((ROWS, COLS), BF16))
        outs.append(jax.ShapeDtypeStruct((H, COLS), F32))
    return pl.pallas_call(
        functools.partial(collect_kernel, bool(more)),
        out_shape=tuple(outs),
        in_specs=[VMEM_SPEC] * (2 + len(more)),
        out_specs=(VMEM_SPEC,) * len(outs),
        compiler_params=params(),
        name="collect_more" if more else "collect_last",
    )(parts, grad, *more)


def shift(value, axis, count, k):
    return lax.ppermute(value, axis, [(s, (s + k) % count) for s in range(count)])


def scatter_kernel(nz, rows, pos, keep, got, *outs):
    for k in range(nz):
        start = pl.multiple_of(lax.rem(pos[1] + k, nz) * rows, 8)
        for l in range(L):
            part = pl.ds(start, rows)
            outs[k][l] = keep[l, part, :] + got[l, part, :]


def place_kernel(nz, rows, pos, *refs):
    out = refs[nz]
    for k in range(nz):
        start = pl.multiple_of(lax.rem(pos[1] - k + nz, nz) * rows, 8)
        for l in range(L):
            out[l, pl.ds(start, rows), :] = refs[k][l]


def reduce_relations(dims, pos, keep, got):
    nx, nz, ny = dims
    rows = keep.shape[1] // nz
    part = jax.ShapeDtypeStruct((L, rows, COLS), F32)
    parts = pl.pallas_call(
        functools.partial(scatter_kernel, nz, rows),
        out_shape=(part,) * nz,
        in_specs=[SMEM_SPEC, VMEM_SPEC, VMEM_SPEC],
        out_specs=(VMEM_SPEC,) * nz,
        compiler_params=params(),
        name="scatter_relations",
    )(pos, keep, got)
    total = parts[0]
    for k in range(1, nz):
        total = total + shift(parts[k], "z", nz, k)
    for axis, count in (("x", nx), ("y", ny)):
        step = 1
        while step < count:
            pairs = [(s, s ^ step) for s in range(count)]
            total = total + lax.ppermute(total, axis, pairs)
            step *= 2
    return total


def gather_relations(nz, pos, total):
    rows = total.shape[1]
    return pl.pallas_call(
        functools.partial(place_kernel, nz, rows),
        out_shape=jax.ShapeDtypeStruct((L, nz * rows, COLS), F32),
        in_specs=[SMEM_SPEC] + [VMEM_SPEC] * nz,
        out_specs=VMEM_SPEC,
        compiler_params=params(),
        name="place_relations",
    )(pos, total, *[shift(total, "z", nz, k) for k in range(1, nz)])


def project(query_vec, relation, scale_factor):
    product = jnp.einsum(
        "qh,rqk->hrk", query_vec, relation.reshape(R, Q, H), precision=EXACT_MATMUL
    )
    return (product.reshape(H, R * H) * scale_factor).astype(BF16)


def whole_rows(core, own, other):
    own, other = (v.reshape(NB_DEV, 1, HB, COLS) for v in (own, other))
    low = jnp.where(core == 0, own, other)
    high = jnp.where(core == 0, other, own)
    return jnp.concatenate([low, high], axis=1).reshape(NB_DEV * BLK, COLS)


def body(dims, node_state, send_list, tile_weight, tile_slot, tile_dst, tile_rel, live_groups,
         query_rel, query_head, rel_table, rel_proj, upd_weight, cotangent):
    nx, nz, ny = dims
    nodes = nx * nz * ny
    half_rows = -(-REL_ROWS // (2 * nz * 8)) * 8 * nz
    x, z, y, core = (lax.axis_index(a) for a in ("x", "z", "y", "c"))
    node = (x * nz + z) * ny + y
    pos = jnp.stack([x, z, y, core]).astype(jnp.int32)
    tiles = tile_weight.shape[2]

    def own_half(rows):
        return lax.dynamic_index_in_dim(
            rows.reshape(NB_DEV, 2, HB, COLS), core, 1, keepdims=False
        ).reshape(ROWS, COLS)

    def swap(value):
        return lax.ppermute(value, "c", SWAP)

    def column_of(copies):
        return lax.all_to_all(copies, "z", 0, 0, tiled=True)

    def spread(rows):
        return jnp.broadcast_to(rows[None], (nz,) + rows.shape)

    state = own_half(node_state)
    listed = jnp.pad(send_list.astype(BF16), ((0, 15), (0, COLS - nodes)))
    column = column_of(spread(jnp.concatenate([state, listed])))

    slot = tile_slot[0, 0]
    slot = ((slot // (nz * ny)) * ny + slot % ny) * nz + (slot // ny) % nz
    live = jnp.broadcast_to(live_groups[0, 0], (tiles,))
    meta = jnp.stack([slot, tile_dst[0, 0], tile_rel[0, 0], live])
    meta = jnp.stack([meta, swap(meta)]).reshape(-1)

    lane_block = jnp.arange(COLS, dtype=jnp.int32) // H
    block_mask = (lane_block[:, None] == lane_block[None, :]).astype(F32)
    upd = [jnp.tile(upd_weight[l], (Q, Q)) * block_mask for l in range(L)]
    upd_t = [u.T for u in upd]
    cot = own_half(cotangent)
    column, meta, upd, upd_t, block_mask, cot = lax.optimization_barrier(
        (column, meta, upd, upd_t, block_mask, cot)
    )
    sends = column[:, ROWS, :nodes].astype(jnp.int32).reshape(-1)
    outgoing = provide(dims, pos, sends, column)
    outgoing, later, query_rel = lax.optimization_barrier((outgoing, pos, query_rel))
    weights = tile_weight[0, 0]
    f_other = swap(lax.dynamic_slice_in_dim(weights, (1 - later[3]) * HB, HB, 1))
    query_vec = query_vectors(rel_table, query_rel)
    row_ids = node * (NB_DEV * BLK) + (
        jnp.arange(NB_DEV, dtype=jnp.int32)[:, None] * BLK
        + core * HB
        + jnp.arange(HB, dtype=jnp.int32)[None, :]
    ).reshape(ROWS)
    matches = (row_ids[:, None] == query_head[None, :]).astype(F32)
    bound = (matches[:, :, None] * query_vec[None, :, :]).reshape(ROWS, COLS)

    received, tables = [], []
    for l in range(L):
        if l:
            copies, vectors = lax.optimization_barrier((spread(state), query_vec))
            table = relation_table(vectors, rel_proj[l])
            column, table = lax.optimization_barrier((column_of(copies), table))
            outgoing = provide(dims, pos, sends, column)
            outgoing, later = lax.optimization_barrier((outgoing, pos))
            b_own, b_send = split_weights(later, weights)
        else:
            table = relation_table(query_vec, rel_proj[l])
        rec_own = lax.all_to_all(outgoing, ("x", "y"), 0, 0, tiled=True)
        if l:
            rec_own, b_own, b_send = lax.optimization_barrier((rec_own, b_own, b_send))
            b_other = swap(b_send)
        else:
            rec_own, table, bound, f_other = lax.optimization_barrier(
                (rec_own, table, bound, f_other)
            )
        tables.append(table)
        rec_own = rec_own.reshape(nodes, HB, COLS)
        received.append(rec_own)
        last = l == L - 1
        more = (cot, upd_t[l], block_mask) if last else ()
        made = forward(
            last, meta, pos, rec_own, swap(rec_own), weights, f_other, tables[l], bound, upd[l],
            state, more,
        )
        state = made[0]
        if last:
            gagg, upd_sum = made[1:]
        else:
            agg0, pre0 = made[1:]

    def core_halves(rel):
        halves = rel.reshape(2, half_rows, COLS)
        return [lax.dynamic_index_in_dim(halves, c, 0, keepdims=False) for c in (core, 1 - core)]

    grad = cot
    relations = [None] * L
    for l in reversed(range(L)):
        sent, rel = backward(
            dims, 2 * half_rows, meta, pos, received[l], b_own, b_other, gagg, swap(gagg),
            tables[l], upd_sum,
        )
        relations[l] = core_halves(rel)
        arrived = lax.all_to_all(sent, ("x", "y"), 0, 0, tiled=True)
        if l == 0:
            keep, send = (jnp.stack([r[i] for r in relations]) for i in range(2))
            total = reduce_relations(dims, pos, keep, swap(send))
            own = gather_relations(nz, pos, total)
            other = swap(own)
            arrived, own, other = lax.optimization_barrier((arrived, own, other))
        combined = combine(dims, pos, sends, arrived)
        if l == 0:
            combined, own, other = lax.optimization_barrier((combined, own, other))
        parts = lax.all_to_all(combined, "z", 0, 0, tiled=True)
        if l == 0:
            low = jnp.where(core == 0, own, other)
            high = jnp.where(core == 0, other, own)
            whole = jnp.concatenate([low, high], axis=1)
            scale_factor = float(nodes * NB_DEV * BLK) ** (-0.5)
            proj = jnp.stack([project(query_vec, whole[k, :R], scale_factor) for k in range(L)])
            upds = whole[:, R8 : R8 + H].reshape(L, H, Q, H).sum(2) * scale_factor
            parts, proj, upds = lax.optimization_barrier((parts, proj, upds))
        more = (pre0, agg0, upd_t[0], block_mask) if l else ()
        made = collect(parts, grad, more)
        grad = made[0]
        if l:
            gagg, upd_sum = made[1:]

    final_state = whole_rows(core, state, swap(state))
    grad_state = whole_rows(core, grad, swap(grad))
    return (final_state, grad_state, proj, upds)


def solution(mesh):
    dims = grid_dims(mesh.shape["node"])
    fine = Mesh(mesh.devices.reshape(*dims, 2), ("x", "z", "y", "c"))
    node = ("x", "z", "y")
    return jax.shard_map(
        functools.partial(body, dims),
        mesh=fine,
        in_specs=(
            P(node, None),
            P(node, None),
            P(node, "c", None, None, None),
            P(node, "c", None),
            P(node, "c", None),
            P(node, "c", None),
            P(node, "c"),
            P(),
            P(),
            P(),
            P(),
            P(),
            P(node, None),
        ),
        out_specs=(P(node, None), P(node, None), P(), P()),
        check_vma=False,
    )
```

```python
import functools

import jax
import jax.numpy as jnp
from jax import lax
from jax.experimental import pallas as pl
from jax.experimental.pallas import tpu as pltpu
from jax.sharding import Mesh
from jax.sharding import PartitionSpec as P

H = 32
R = 535
BLK = 128
HB = BLK // 2
Q = 4
L = 2
GROUP = 16
NB_DEV = 4
COLS = Q * H
ROWS = NB_DEV * HB
R8 = 536
REL_ROWS = R8 + H
F32 = jnp.float32
BF16 = jnp.bfloat16
EXACT_MATMUL = lax.Precision.HIGHEST
VMEM_LIMIT = 48 * 1024 * 1024
SWAP = [(0, 1), (1, 0)]
SMEM_SPEC = pl.BlockSpec(memory_space=pltpu.SMEM)
VMEM_SPEC = pl.BlockSpec(memory_space=pltpu.VMEM)
ANY_SPEC = pl.BlockSpec(memory_space=pl.ANY)
HBM_SPEC = pl.BlockSpec(memory_space=pltpu.HBM)
WIDE = R8 * H
RM = BLK // H


def grid_dims(node_count):
    if node_count == 128:
        return (4, 8, 4)
    return (2, node_count // 4, 2)


def params():
    return pltpu.CompilerParams(vmem_limit_bytes=VMEM_LIMIT)


def query_vectors(rel_table, query_rel):
    relation_ids = jnp.arange(R, dtype=jnp.int32)
    picked = (query_rel[:, None] == relation_ids[None, :]).astype(F32)
    return jnp.dot(picked, rel_table, precision=EXACT_MATMUL)


def lanes_of(shape):
    return lax.broadcasted_iota(jnp.int32, shape, 1) // H


def table_kernel(flat, table, rows):
    for j in range(R8 // RM):
        rows[:, j, :] = flat[:, j * BLK : (j + 1) * BLK]
    lane = lanes_of(rows.shape[1:])
    for m in range(RM):
        made = jnp.zeros(rows.shape[1:], F32)
        for q in range(Q):
            made = jnp.where(lane == q, pltpu.roll(rows[q], (q - m) * H % COLS, 1), made)
        table[pl.ds(m, R8 // RM, stride=RM), :] = made[: R8 // RM]


def flat_kernel(table, flat, rows):
    lane = lanes_of(rows.shape[1:])
    count = rows.shape[1]
    for q in range(Q):
        rows[q] = jnp.zeros((count, COLS), F32)
    for m in range(RM):
        read = table[pl.ds(m, count, stride=RM), :]
        for q in range(Q):
            rows[q] = jnp.where(lane == m, pltpu.roll(read, (m - q) * H % COLS, 1), rows[q])
    for j in range(R8 // RM):
        flat[:, j * BLK : (j + 1) * BLK] = rows[:, j, :]


def relayout(kernel, shape, value):
    return pl.pallas_call(
        kernel,
        out_shape=jax.ShapeDtypeStruct(shape, F32),
        in_specs=[VMEM_SPEC],
        out_specs=VMEM_SPEC,
        scratch_shapes=[pltpu.VMEM((Q, -(-R8 // (8 * RM)) * 8, COLS), F32)],
        compiler_params=params(),
        cost_estimate=pl.CostEstimate(flops=0, bytes_accessed=4 << 20, transcendentals=0),
        name=kernel.__name__,
    )(value)


def relation_table(query_vec, proj):
    flat = jnp.dot(query_vec, proj.astype(F32), precision=EXACT_MATMUL)
    return relayout(table_kernel, (R8, COLS), jnp.pad(flat, ((0, 0), (0, WIDE - R * H))))


def split_kernel(pos, w_ref, keep, send):
    core = pos[3]
    for t in range(w_ref.shape[0]):
        flipped = w_ref[t].T
        low, high = flipped[:HB], flipped[HB:]
        keep[t] = jnp.where(core == 0, low, high)
        send[t] = jnp.where(core == 0, high, low)


def split_weights(pos, weights):
    tiles = weights.shape[0]
    half = jax.ShapeDtypeStruct((tiles, HB, BLK), BF16)
    spec = pl.BlockSpec((GROUP, HB, BLK), lambda g: (g, 0, 0))
    return pl.pallas_call(
        split_kernel,
        out_shape=(half,) * 2,
        grid=(tiles // GROUP,),
        in_specs=[SMEM_SPEC, pl.BlockSpec((GROUP, BLK, BLK), lambda g: (g, 0, 0))],
        out_specs=[spec] * 2,
        compiler_params=params(),
        cost_estimate=pl.CostEstimate(
            flops=0, bytes_accessed=tiles * BLK * BLK * 2 * 2, transcendentals=0
        ),
        name="split_weights",
    )(pos, weights)


def provide_kernel(dims, pos, sends, column, out, blocks, sems):
    nx, nz, ny = dims
    z = pos[1]
    nodes = nx * nz * ny
    copies = []
    for d in range(nx * ny):
        reader = (d // ny) * (nz * ny) + z * ny + d % ny
        for owner in range(nz):
            block = sends[owner * nodes + reader]
            start = pl.multiple_of(block * HB, HB)
            blocks[d, owner] = column[owner, pl.ds(start, HB), :]
        copies.append(pltpu.make_async_copy(blocks.at[d], out.at[d], sems.at[d]))
        copies[-1].start()
    for copy in copies:
        copy.wait()


def provide(dims, pos, sends, column):
    nx, nz, ny = dims
    shape = (nx * ny, nz, HB, COLS)
    return pl.pallas_call(
        functools.partial(provide_kernel, dims),
        out_shape=pltpu.HBM(shape, BF16),
        in_specs=[SMEM_SPEC, SMEM_SPEC, VMEM_SPEC],
        out_specs=HBM_SPEC,
        scratch_shapes=[pltpu.VMEM(shape, BF16), pltpu.SemaphoreType.DMA((nx * ny,))],
        compiler_params=params(),
        name="provide",
    )(pos, sends, column)


def start_weights(meta, tiles, weights, buffer, sems):
    groups = tiles // GROUP
    for source in range(2):
        live = meta[(source * 4 + 3) * tiles]
        for g in range(groups):

            @pl.when(g < live)
            def _(source=source, g=g):
                pltpu.make_async_copy(
                    weights[source](pl.ds(g * GROUP, GROUP)),
                    buffer.at[source * groups + g],
                    sems.at[source * groups + g],
                ).start()


def over_tiles(meta, tiles, weights, buffer, sems, one_tile):
    groups = tiles // GROUP
    for source in range(2):
        live = meta[(source * 4 + 3) * tiles]
        base = source * 4 * tiles

        def one_group(g, carry, source=source, base=base):
            place = source * groups + g
            pltpu.make_async_copy(
                weights[source](pl.ds(g * GROUP, GROUP)),
                buffer.at[place],
                sems.at[place],
            ).wait()
            for t in range(GROUP):
                at = base + g * GROUP + t
                one_tile(
                    buffer[place, t],
                    meta[at],
                    meta[at + tiles],
                    meta[at + 2 * tiles],
                )
            return carry

        lax.fori_loop(0, live, one_group, 0)


def update_terms(aggregate, grad_pre, block_mask):
    product = jnp.dot(aggregate.T, grad_pre, precision=EXACT_MATMUL, preferred_element_type=F32)
    product = product * block_mask
    total = product[:H]
    for q in range(1, Q):
        total = total + product[q * H : (q + 1) * H]
    return total


def before_backward(grad, pre, aggregate, upd_t, block_mask, gagg_ref, upd_ref):
    sigma = jax.nn.sigmoid(pre)
    grad_pre = grad * (sigma * (1.0 + pre * (1.0 - sigma)))
    gagg_ref[...] = jnp.dot(
        grad_pre, upd_t, precision=EXACT_MATMUL, preferred_element_type=F32
    ).astype(BF16)
    upd_ref[...] = update_terms(aggregate, grad_pre, block_mask)


def forward_kernel(last, tiles, meta, pos, rec_own, rec_other, w_own, w_other, table, bound,
                   upd, state, *refs):
    if last:
        cotangent, upd_t, block_mask = refs[:3]
        next_ref, gagg_ref, upd_ref, rec, buffer, acc, w_sems, r_sems = refs[3:]
    else:
        next_ref, aux_ref, rec, buffer, acc, w_sems, r_sems, aux = refs
    own = pl.multiple_of(pos[3] * HB, HB)
    other = pl.multiple_of((1 - pos[3]) * HB, HB)
    copies = [
        pltpu.make_async_copy(rec_own, rec.at[:, pl.ds(own, HB), :], r_sems.at[0]),
        pltpu.make_async_copy(rec_other, rec.at[:, pl.ds(other, HB), :], r_sems.at[1]),
    ]
    for copy in copies:
        copy.start()
    weights = [lambda g, w=w: w.at[g, pl.ds(own, HB), :] for w in (w_own, w_other)]
    start_weights(meta, tiles, weights, buffer, w_sems)
    acc[...] = jnp.zeros_like(acc)
    for copy in copies:
        copy.wait()

    def one_tile(weight, slot, dst, rel):
        message = jnp.dot(weight, rec[slot], preferred_element_type=F32)
        acc[dst] = acc[dst] + message * table[pl.ds(rel, 1), :]

    over_tiles(meta, tiles, weights, buffer, w_sems, one_tile)
    aggregate = acc[...].reshape(ROWS, COLS) + bound[...]
    pre = jnp.dot(aggregate, upd[...], precision=EXACT_MATMUL, preferred_element_type=F32)
    next_ref[...] = (state[...].astype(F32) + pre * jax.nn.sigmoid(pre)).astype(BF16)
    if last:
        before_backward(
            cotangent[...].astype(F32), pre, aggregate, upd_t[...], block_mask[...],
            gagg_ref, upd_ref,
        )
    else:
        aux[0] = aggregate
        aux[1] = pre
        kept = pltpu.make_async_copy(aux, aux_ref, r_sems.at[2])
        kept.start()
        kept.wait()


def forward(last, meta, pos, rec_own, rec_other, w_own, w_other, table, bound, upd, state, more):
    slots, tiles = rec_own.shape[0], w_own.shape[0]
    places = 2 * (tiles // GROUP)
    rows16 = jax.ShapeDtypeStruct((ROWS, COLS), BF16)
    pair = pltpu.HBM((2, ROWS, COLS), F32)
    if last:
        outs = (rows16, rows16, jax.ShapeDtypeStruct((H, COLS), F32))
    else:
        outs = (rows16, pair)
    return pl.pallas_call(
        functools.partial(forward_kernel, last, tiles),
        out_shape=outs,
        in_specs=[SMEM_SPEC, SMEM_SPEC] + [ANY_SPEC] * 4 + [VMEM_SPEC] * (4 + len(more)),
        out_specs=(VMEM_SPEC,) * 3 if last else (VMEM_SPEC, HBM_SPEC),
        scratch_shapes=[
            pltpu.VMEM((slots, BLK, COLS), BF16),
            pltpu.VMEM((places, GROUP, HB, BLK), BF16),
            pltpu.VMEM((NB_DEV, HB, COLS), F32),
            pltpu.SemaphoreType.DMA((places,)),
            pltpu.SemaphoreType.DMA((3,)),
        ]
        + ([] if last else [pltpu.VMEM((2, ROWS, COLS), F32)]),
        compiler_params=params(),
        name="forward_last" if last else "forward_first",
    )(meta, pos, rec_own, rec_other, w_own, w_other, table, bound, upd, state, *more)


def backward_kernel(dims, tiles, chunk, meta, pos, rec_own, w_own, w_other, gagg_own,
                    gagg_other, table, upd_sum, *refs):
    passed, refs = refs[:-8], refs[-8:]
    out, rec, buffer, slot_acc, rel_acc, gagg, w_sems, r_sem = refs
    nx, nz, ny = dims
    copy = pltpu.make_async_copy(rec_own, rec, r_sem.at[0])
    copy.start()
    weights = (lambda g: w_own.at[g], lambda g: w_other.at[g])
    start_weights(meta, tiles, weights, buffer, w_sems)
    own = pl.multiple_of(pos[3] * HB, HB)
    other = pl.multiple_of((1 - pos[3]) * HB, HB)
    gagg[:, pl.ds(own, HB), :] = gagg_own[...].reshape(NB_DEV, HB, COLS)
    gagg[:, pl.ds(other, HB), :] = gagg_other[...].reshape(NB_DEV, HB, COLS)
    rel_acc[...] = jnp.zeros_like(rel_acc)
    rel_acc[R8 : R8 + H, :] = upd_sum[...]

    def clear(d, carry):
        slot_acc[pl.ds(d * nz, nz)] = jnp.zeros((nz, HB, COLS), F32)
        return carry

    lax.fori_loop(0, nx * ny, clear, 0)
    copy.wait()

    def one_tile(weight, slot, dst, rel):
        back = jnp.dot(weight, gagg[dst], preferred_element_type=F32)
        row = pl.ds(rel, 1)
        slot_acc[slot] = slot_acc[slot] + back * table[row, :]
        terms = jnp.sum(back * rec[slot].astype(F32), axis=0, keepdims=True)
        rel_acc[row, :] = rel_acc[row, :] + terms

    over_tiles(meta, tiles, weights, buffer, w_sems, one_tile)

    def put(d, carry):
        out[d, : nz * HB, :] = slot_acc[pl.ds(d * nz, nz)].reshape(nz * HB, COLS).astype(BF16)
        start = pl.multiple_of(d * chunk, 16)
        out[d, nz * HB : nz * HB + chunk, :] = rel_acc[pl.ds(start, chunk), :].astype(BF16)
        for part in passed:
            out[d, nz * HB + chunk :, :] = part[...].astype(BF16)
        return carry

    lax.fori_loop(0, nx * ny, put, 0)


def backward(dims, chunk, meta, pos, rec_own, w_own, w_other, gagg_own, gagg_other, table, upd_sum,
             passed):
    nx, nz, ny = dims
    slots, tiles = rec_own.shape[0], w_own.shape[0]
    places = 2 * (tiles // GROUP)
    return pl.pallas_call(
        functools.partial(backward_kernel, dims, tiles, chunk),
        out_shape=jax.ShapeDtypeStruct(
            (nx * ny, nz * HB + chunk * (1 + len(passed)), COLS), BF16
        ),
        in_specs=[SMEM_SPEC, SMEM_SPEC] + [ANY_SPEC] * 3 + [VMEM_SPEC] * (4 + len(passed)),
        out_specs=VMEM_SPEC,
        scratch_shapes=[
            pltpu.VMEM((slots, HB, COLS), BF16),
            pltpu.VMEM((places, GROUP, HB, BLK), BF16),
            pltpu.VMEM((slots, HB, COLS), F32),
            pltpu.VMEM((nx * ny * chunk, COLS), F32),
            pltpu.VMEM((NB_DEV, BLK, COLS), BF16),
            pltpu.SemaphoreType.DMA((places,)),
            pltpu.SemaphoreType.DMA((1,)),
        ],
        compiler_params=params(),
        name="backward",
    )(meta, pos, rec_own, w_own, w_other, gagg_own, gagg_other, table, upd_sum, *passed)


def combine_kernel(dims, chunk, pos, sends, arrived, out, *refs):
    acc = refs[-1]
    nx, nz, ny = dims
    z = pos[1]
    nodes = nx * nz * ny
    acc[...] = jnp.zeros_like(acc)
    rel = jnp.zeros((chunk, COLS), F32)
    for s in range(nx * ny):
        sender = (s // ny) * (nz * ny) + z * ny + s % ny
        for owner in range(nz):
            block = sends[owner * nodes + sender]
            acc[owner, block] = acc[owner, block] + arrived[
                s, owner * HB : (owner + 1) * HB, :
            ].astype(F32)
        rel = rel + arrived[s, nz * HB : nz * HB + chunk, :].astype(F32)
        for whole in refs[:-1]:
            whole[s * chunk : (s + 1) * chunk, :] = arrived[s, nz * HB + chunk :, :].astype(F32)
    for owner in range(nz):
        out[owner, :ROWS, :] = acc[owner].reshape(ROWS, COLS).astype(BF16)
        out[owner, ROWS:, :] = rel.astype(BF16)


def combine(dims, chunk, pos, sends, arrived):
    nx, nz, ny = dims
    outs = [jax.ShapeDtypeStruct((nz, ROWS + chunk, COLS), BF16)]
    if arrived.shape[1] > nz * HB + chunk:
        outs.append(jax.ShapeDtypeStruct((nx * ny * chunk, COLS), F32))
    return pl.pallas_call(
        functools.partial(combine_kernel, dims, chunk),
        out_shape=outs,
        in_specs=[SMEM_SPEC, SMEM_SPEC, VMEM_SPEC],
        out_specs=[VMEM_SPEC] * len(outs),
        scratch_shapes=[pltpu.VMEM((nz, NB_DEV, HB, COLS), F32)],
        compiler_params=params(),
        name="combine",
    )(pos, sends, arrived)


def collect_kernel(more, parts, *refs):
    if more:
        aux_hbm, upd_t, block_mask, aux, sem = refs[1], refs[2], refs[3], refs[-2], refs[-1]
        copy = pltpu.make_async_copy(aux_hbm, aux, sem.at[0])
        copy.start()
    total = parts[0].astype(F32)
    for k in range(1, parts.shape[0]):
        total = total + parts[k].astype(F32)
    grad = refs[0][...].astype(F32) + total[:ROWS]
    if more:
        grad_ref, rel_ref, gagg_ref, upd_ref = refs[4:-2]
        copy.wait()
        before_backward(grad, aux[1], aux[0], upd_t[...], block_mask[...], gagg_ref, upd_ref)
    else:
        grad_ref, rel_ref = refs[1:]
    grad_ref[...] = grad
    rel_ref[...] = total[ROWS:]


def collect(chunk, parts, grad, more):
    outs = [jax.ShapeDtypeStruct((ROWS, COLS), F32), jax.ShapeDtypeStruct((chunk, COLS), F32)]
    in_specs = [VMEM_SPEC, VMEM_SPEC]
    scratch = []
    if more:
        outs.append(jax.ShapeDtypeStruct((ROWS, COLS), BF16))
        outs.append(jax.ShapeDtypeStruct((H, COLS), F32))
        in_specs += [HBM_SPEC, VMEM_SPEC, VMEM_SPEC]
        scratch = [pltpu.VMEM((2, ROWS, COLS), F32), pltpu.SemaphoreType.DMA((1,))]
    return pl.pallas_call(
        functools.partial(collect_kernel, bool(more)),
        out_shape=tuple(outs),
        in_specs=in_specs,
        out_specs=(VMEM_SPEC,) * len(outs),
        scratch_shapes=scratch,
        compiler_params=params(),
        name="collect_more" if more else "collect_last",
    )(parts, grad, *more)


def gather_relations(dims, rel):
    count = dims[0] * dims[2]
    copies = jnp.broadcast_to(rel[None], (count,) + rel.shape)
    parts = lax.all_to_all(copies, ("x", "y"), 0, 0, tiled=True)
    return parts.reshape(count * rel.shape[0], COLS)


def project(query_vec, relation, scale_factor):
    flat = relayout(flat_kernel, (Q, WIDE), relation)
    product = jnp.dot(query_vec.T, flat, precision=EXACT_MATMUL)
    return (product[:, : R * H] * scale_factor).astype(BF16)


def update_sum(relation, scale_factor):
    return relation[R8 : R8 + H].reshape(H, Q, H).sum(1) * scale_factor


def whole_rows(core, own, other):
    own, other = (v.reshape(NB_DEV, 1, HB, COLS) for v in (own, other))
    low = jnp.where(core == 0, own, other)
    high = jnp.where(core == 0, other, own)
    return jnp.concatenate([low, high], axis=1).reshape(NB_DEV * BLK, COLS)


def body(dims, node_state, send_list, tile_weight, tile_slot, tile_dst, tile_rel, live_groups,
         query_rel, query_head, rel_table, rel_proj, upd_weight, cotangent):
    nx, nz, ny = dims
    nodes = nx * nz * ny
    chunk = -(-REL_ROWS // (nx * ny * 16)) * 16
    x, z, y, core = (lax.axis_index(a) for a in ("x", "z", "y", "c"))
    node = (x * nz + z) * ny + y
    pos = jnp.stack([x, z, y, core]).astype(jnp.int32)
    tiles = tile_weight.shape[2]

    def own_half(rows):
        return lax.dynamic_index_in_dim(
            rows.reshape(NB_DEV, 2, HB, COLS), core, 1, keepdims=False
        ).reshape(ROWS, COLS)

    def swap(value):
        return lax.ppermute(value, "c", SWAP)

    def column_of(copies):
        return lax.all_to_all(copies, "z", 0, 0, tiled=True)

    def spread(rows):
        return jnp.broadcast_to(rows[None], (nz,) + rows.shape)

    state = own_half(node_state)
    listed = jnp.pad(send_list.astype(BF16), ((0, 15), (0, COLS - nodes)))
    column = column_of(spread(jnp.concatenate([state, listed])))

    slot = tile_slot[0, 0]
    slot = ((slot // (nz * ny)) * ny + slot % ny) * nz + (slot // ny) % nz
    live = jnp.broadcast_to(live_groups[0, 0], (tiles,))
    meta = jnp.stack([slot, tile_dst[0, 0], tile_rel[0, 0], live])
    meta = jnp.stack([meta, swap(meta)]).reshape(-1)

    lane_block = jnp.arange(COLS, dtype=jnp.int32) // H
    block_mask = (lane_block[:, None] == lane_block[None, :]).astype(F32)
    upd = [jnp.tile(upd_weight[l], (Q, Q)) * block_mask for l in range(L)]
    upd_t = [u.T for u in upd]
    cot = own_half(cotangent)
    query_vec = query_vectors(rel_table, query_rel)
    first_table = relation_table(query_vec, rel_proj[0])
    weights = tile_weight[0, 0]
    f_other = swap(weights)
    held = (column, meta, upd, upd_t, block_mask, cot, first_table, f_other)
    held = lax.optimization_barrier(held)
    column, meta, upd, upd_t, block_mask, cot, first_table, f_other = held
    sends = column[:, ROWS, :nodes].astype(jnp.int32).reshape(-1)
    outgoing = provide(dims, pos, sends, column)
    outgoing, later = lax.optimization_barrier((outgoing, pos))
    b_own, b_send = split_weights(later, weights)
    row_ids = node * (NB_DEV * BLK) + (
        jnp.arange(NB_DEV, dtype=jnp.int32)[:, None] * BLK
        + core * HB
        + jnp.arange(HB, dtype=jnp.int32)[None, :]
    ).reshape(ROWS)
    matches = (row_ids[:, None] == query_head[None, :]).astype(F32)
    bound = (matches[:, :, None] * query_vec[None, :, :]).reshape(ROWS, COLS)

    received, tables = [], []
    for l in range(L):
        if l:
            column, b_other = lax.optimization_barrier((column_of(spread(state)), b_other))
            outgoing = provide(dims, pos, sends, column)
            outgoing, vectors = lax.optimization_barrier((outgoing, query_vec))
        else:
            table = first_table
        rec_own = lax.all_to_all(outgoing, ("x", "y"), 0, 0, tiled=True)
        if l:
            table = relation_table(vectors, rel_proj[l])
            rec_own, table = lax.optimization_barrier((rec_own, table))
        else:
            rec_own, bound, b_own, b_send = lax.optimization_barrier(
                (rec_own, bound, b_own, b_send)
            )
        tables.append(table)
        rec_own = rec_own.reshape(nodes, HB, COLS)
        received.append(rec_own)
        last = l == L - 1
        more = (cot, upd_t[l], block_mask) if last else ()
        rec_other = swap(rec_own)
        if l == 0:
            rec_other, b_send = lax.optimization_barrier((rec_other, b_send))
            b_other = swap(b_send)
        made = forward(
            last, meta, pos, rec_own, rec_other, weights, f_other, tables[l], bound, upd[l],
            state, more,
        )
        state = made[0]
        if last:
            gagg, upd_sum = made[1:]
        else:
            aux = pltpu.with_memory_space_constraint(made[1], pltpu.HBM)

    grad = cot
    passed = ()
    scale_factor = float(nodes * NB_DEV * BLK) ** (-0.5)
    for l in reversed(range(L)):
        sent = backward(
            dims, chunk, meta, pos, received[l], b_own, b_other, gagg, swap(gagg), tables[l],
            upd_sum, passed,
        )
        arrived = lax.all_to_all(sent, ("x", "y"), 0, 0, tiled=True)
        combined, *whole = combine(dims, chunk, pos, sends, arrived)
        parts = lax.all_to_all(combined, "z", 0, 0, tiled=True)
        if whole:
            relation = whole[0] + swap(whole[0])
            last_proj = project(query_vec, relation, scale_factor)
            last_upd = update_sum(relation, scale_factor)
            parts, last_proj, last_upd = lax.optimization_barrier((parts, last_proj, last_upd))
        more = (aux, upd_t[0], block_mask) if l else ()
        made = collect(chunk, parts, grad, more)
        grad, rel = made[:2]
        if l:
            gagg, upd_sum = made[2:]
        passed = (rel,) if l else ()
    relation = gather_relations(dims, rel + swap(rel))

    proj = jnp.stack([project(query_vec, relation, scale_factor), last_proj])
    upds = jnp.stack([update_sum(relation, scale_factor), last_upd])
    final_state = whole_rows(core, state, swap(state))
    grad_state = whole_rows(core, grad, swap(grad))
    return (
        final_state,
        grad_state,
        proj,
        upds,
    )


def solution(mesh):
    dims = grid_dims(mesh.shape["node"])
    fine = Mesh(mesh.devices.reshape(*dims, 2), ("x", "z", "y", "c"))
    node = ("x", "z", "y")
    return jax.shard_map(
        functools.partial(body, dims),
        mesh=fine,
        in_specs=(
            P(node, None),
            P(node, None),
            P(node, "c", None, None, None),
            P(node, "c", None),
            P(node, "c", None),
            P(node, "c", None),
            P(node, "c"),
            P(),
            P(),
            P(),
            P(),
            P(),
            P(node, None),
        ),
        out_specs=(P(node, None), P(node, None), P(), P()),
        check_vma=False,
    )
```

```python
import functools

import jax
import jax.numpy as jnp
from jax import lax
from jax.experimental import pallas as pl
from jax.experimental.pallas import tpu as pltpu
from jax.sharding import Mesh
from jax.sharding import PartitionSpec as P

H = 32
R = 535
BLK = 128
HB = BLK // 2
Q = 4
L = 2
GROUP = 16
NB_DEV = 4
COLS = Q * H
ROWS = NB_DEV * HB
R8 = 536
REL_ROWS = R8 + H
F32 = jnp.float32
BF16 = jnp.bfloat16
EXACT_MATMUL = lax.Precision.HIGHEST
VMEM_LIMIT = 48 * 1024 * 1024
SWAP = [(0, 1), (1, 0)]
SMEM_SPEC = pl.BlockSpec(memory_space=pltpu.SMEM)
VMEM_SPEC = pl.BlockSpec(memory_space=pltpu.VMEM)
ANY_SPEC = pl.BlockSpec(memory_space=pl.ANY)
HBM_SPEC = pl.BlockSpec(memory_space=pltpu.HBM)
WIDE = R8 * H
RM = BLK // H


def grid_dims(node_count):
    if node_count == 128:
        return (4, 8, 4)
    return (2, node_count // 4, 2)


def params():
    return pltpu.CompilerParams(vmem_limit_bytes=VMEM_LIMIT)


def query_vectors(rel_table, query_rel):
    relation_ids = jnp.arange(R, dtype=jnp.int32)
    picked = (query_rel[:, None] == relation_ids[None, :]).astype(F32)
    return jnp.dot(picked, rel_table, precision=EXACT_MATMUL)


def lanes_of(shape):
    return lax.broadcasted_iota(jnp.int32, shape, 1) // H


def table_kernel(flat, table, rows):
    for j in range(R8 // RM):
        rows[:, j, :] = flat[:, j * BLK : (j + 1) * BLK]
    lane = lanes_of(rows.shape[1:])
    for m in range(RM):
        made = jnp.zeros(rows.shape[1:], F32)
        for q in range(Q):
            made = jnp.where(lane == q, pltpu.roll(rows[q], (q - m) * H % COLS, 1), made)
        table[pl.ds(m, R8 // RM, stride=RM), :] = made[: R8 // RM]


def flat_kernel(table, flat, rows):
    lane = lanes_of(rows.shape[1:])
    count = rows.shape[1]
    for q in range(Q):
        rows[q] = jnp.zeros((count, COLS), F32)
    for m in range(RM):
        read = table[pl.ds(m, count, stride=RM), :]
        for q in range(Q):
            rows[q] = jnp.where(lane == m, pltpu.roll(read, (m - q) * H % COLS, 1), rows[q])
    for j in range(R8 // RM):
        flat[:, j * BLK : (j + 1) * BLK] = rows[:, j, :]


def relayout(kernel, shape, value):
    return pl.pallas_call(
        kernel,
        out_shape=jax.ShapeDtypeStruct(shape, F32),
        in_specs=[VMEM_SPEC],
        out_specs=VMEM_SPEC,
        scratch_shapes=[pltpu.VMEM((Q, -(-R8 // (8 * RM)) * 8, COLS), F32)],
        compiler_params=params(),
        cost_estimate=pl.CostEstimate(flops=0, bytes_accessed=4 << 20, transcendentals=0),
        name=kernel.__name__,
    )(value)


def relation_table(query_vec, proj):
    flat = jnp.dot(query_vec, proj.astype(F32), precision=EXACT_MATMUL)
    return relayout(table_kernel, (R8, COLS), jnp.pad(flat, ((0, 0), (0, WIDE - R * H))))


def split_kernel(pos, w_ref, keep, send):
    core = pos[3]
    for t in range(w_ref.shape[0]):
        flipped = w_ref[t].T
        low, high = flipped[:HB], flipped[HB:]
        keep[t] = jnp.where(core == 0, low, high)
        send[t] = jnp.where(core == 0, high, low)


def split_weights(pos, weights):
    tiles = weights.shape[0]
    half = jax.ShapeDtypeStruct((tiles, HB, BLK), BF16)
    spec = pl.BlockSpec((GROUP, HB, BLK), lambda g: (g, 0, 0))
    return pl.pallas_call(
        split_kernel,
        out_shape=(half,) * 2,
        grid=(tiles // GROUP,),
        in_specs=[SMEM_SPEC, pl.BlockSpec((GROUP, BLK, BLK), lambda g: (g, 0, 0))],
        out_specs=[spec] * 2,
        compiler_params=params(),
        cost_estimate=pl.CostEstimate(
            flops=0, bytes_accessed=tiles * BLK * BLK * 2 * 2, transcendentals=0
        ),
        name="split_weights",
    )(pos, weights)


def provide_kernel(dims, pos, sends, *refs):
    nx, nz, ny = dims
    column, (out, blocks, sems) = refs[:nz], refs[nz:]
    z = pos[1]
    nodes = nx * nz * ny
    copies = []
    for d in range(nx * ny):
        reader = (d // ny) * (nz * ny) + z * ny + d % ny
        for k in range(nz):
            block = sends[k * nodes + reader]
            start = pl.multiple_of(block * HB, HB)
            blocks[d, lax.rem(z - k + nz, nz)] = column[k][pl.ds(start, HB), :]
        copies.append(pltpu.make_async_copy(blocks.at[d], out.at[d], sems.at[d]))
        copies[-1].start()
    for copy in copies:
        copy.wait()


def provide(dims, pos, sends, column):
    nx, nz, ny = dims
    shape = (nx * ny, nz, HB, COLS)
    return pl.pallas_call(
        functools.partial(provide_kernel, dims),
        out_shape=pltpu.HBM(shape, BF16),
        in_specs=[SMEM_SPEC, SMEM_SPEC] + [VMEM_SPEC] * nz,
        out_specs=HBM_SPEC,
        scratch_shapes=[pltpu.VMEM(shape, BF16), pltpu.SemaphoreType.DMA((nx * ny,))],
        compiler_params=params(),
        name="provide",
    )(pos, sends, *column)


def start_weights(meta, tiles, weights, buffer, sems):
    groups = tiles // GROUP
    for source in range(2):
        live = meta[(source * 4 + 3) * tiles]
        for g in range(groups):

            @pl.when(g < live)
            def _(source=source, g=g):
                pltpu.make_async_copy(
                    weights[source](pl.ds(g * GROUP, GROUP)),
                    buffer.at[source * groups + g],
                    sems.at[source * groups + g],
                ).start()


def over_tiles(meta, tiles, weights, buffer, sems, one_tile):
    groups = tiles // GROUP
    for source in range(2):
        live = meta[(source * 4 + 3) * tiles]
        base = source * 4 * tiles

        def one_group(g, carry, source=source, base=base):
            place = source * groups + g
            pltpu.make_async_copy(
                weights[source](pl.ds(g * GROUP, GROUP)),
                buffer.at[place],
                sems.at[place],
            ).wait()
            for t in range(GROUP):
                at = base + g * GROUP + t
                one_tile(
                    buffer[place, t],
                    meta[at],
                    meta[at + tiles],
                    meta[at + 2 * tiles],
                )
            return carry

        lax.fori_loop(0, live, one_group, 0)


def update_terms(aggregate, grad_pre, block_mask):
    product = jnp.dot(aggregate.T, grad_pre, precision=EXACT_MATMUL, preferred_element_type=F32)
    product = product * block_mask
    total = product[:H]
    for q in range(1, Q):
        total = total + product[q * H : (q + 1) * H]
    return total


def before_backward(grad, pre, aggregate, upd_t, block_mask, gagg_ref, upd_ref):
    sigma = jax.nn.sigmoid(pre)
    grad_pre = grad * (sigma * (1.0 + pre * (1.0 - sigma)))
    gagg_ref[...] = jnp.dot(
        grad_pre, upd_t, precision=EXACT_MATMUL, preferred_element_type=F32
    ).astype(BF16)
    upd_ref[...] = update_terms(aggregate, grad_pre, block_mask)


def forward_kernel(last, tiles, meta, pos, rec_own, rec_other, w_own, w_other, table, bound,
                   upd, state, *refs):
    if last:
        cotangent, upd_t, block_mask = refs[:3]
        next_ref, gagg_ref, upd_ref, rec, buffer, acc, w_sems, r_sems = refs[3:]
    else:
        next_ref, aux_ref, rec, buffer, acc, w_sems, r_sems, aux = refs
    own = pl.multiple_of(pos[3] * HB, HB)
    other = pl.multiple_of((1 - pos[3]) * HB, HB)
    copies = [
        pltpu.make_async_copy(rec_own, rec.at[:, pl.ds(own, HB), :], r_sems.at[0]),
        pltpu.make_async_copy(rec_other, rec.at[:, pl.ds(other, HB), :], r_sems.at[1]),
    ]
    for copy in copies:
        copy.start()
    weights = [lambda g, w=w: w.at[g, pl.ds(own, HB), :] for w in (w_own, w_other)]
    start_weights(meta, tiles, weights, buffer, w_sems)
    acc[...] = jnp.zeros_like(acc)
    for copy in copies:
        copy.wait()

    def one_tile(weight, slot, dst, rel):
        message = jnp.dot(weight, rec[slot], preferred_element_type=F32)
        acc[dst] = acc[dst] + message * table[pl.ds(rel, 1), :]

    over_tiles(meta, tiles, weights, buffer, w_sems, one_tile)
    aggregate = acc[...].reshape(ROWS, COLS) + bound[...]
    pre = jnp.dot(aggregate, upd[...], precision=EXACT_MATMUL, preferred_element_type=F32)
    next_ref[...] = (state[...].astype(F32) + pre * jax.nn.sigmoid(pre)).astype(BF16)
    if last:
        before_backward(
            cotangent[...].astype(F32), pre, aggregate, upd_t[...], block_mask[...],
            gagg_ref, upd_ref,
        )
    else:
        aux[0] = aggregate
        aux[1] = pre
        kept = pltpu.make_async_copy(aux, aux_ref, r_sems.at[2])
        kept.start()
        kept.wait()


def forward(last, meta, pos, rec_own, rec_other, w_own, w_other, table, bound, upd, state, more):
    slots, tiles = rec_own.shape[0], w_own.shape[0]
    places = 2 * (tiles // GROUP)
    rows16 = jax.ShapeDtypeStruct((ROWS, COLS), BF16)
    pair = pltpu.HBM((2, ROWS, COLS), F32)
    if last:
        outs = (rows16, rows16, jax.ShapeDtypeStruct((H, COLS), F32))
    else:
        outs = (rows16, pair)
    return pl.pallas_call(
        functools.partial(forward_kernel, last, tiles),
        out_shape=outs,
        in_specs=[SMEM_SPEC, SMEM_SPEC] + [ANY_SPEC] * 4 + [VMEM_SPEC] * (4 + len(more)),
        out_specs=(VMEM_SPEC,) * 3 if last else (VMEM_SPEC, HBM_SPEC),
        scratch_shapes=[
            pltpu.VMEM((slots, BLK, COLS), BF16),
            pltpu.VMEM((places, GROUP, HB, BLK), BF16),
            pltpu.VMEM((NB_DEV, HB, COLS), F32),
            pltpu.SemaphoreType.DMA((places,)),
            pltpu.SemaphoreType.DMA((3,)),
        ]
        + ([] if last else [pltpu.VMEM((2, ROWS, COLS), F32)]),
        compiler_params=params(),
        name="forward_last" if last else "forward_first",
    )(meta, pos, rec_own, rec_other, w_own, w_other, table, bound, upd, state, *more)


def backward_kernel(dims, tiles, chunk, meta, pos, rec_own, w_own, w_other, gagg_own,
                    gagg_other, table, upd_sum, *refs):
    passed, refs = refs[:-8], refs[-8:]
    out, rec, buffer, slot_acc, rel_acc, gagg, w_sems, r_sem = refs
    nx, nz, ny = dims
    copy = pltpu.make_async_copy(rec_own, rec, r_sem.at[0])
    copy.start()
    weights = (lambda g: w_own.at[g], lambda g: w_other.at[g])
    start_weights(meta, tiles, weights, buffer, w_sems)
    own = pl.multiple_of(pos[3] * HB, HB)
    other = pl.multiple_of((1 - pos[3]) * HB, HB)
    gagg[:, pl.ds(own, HB), :] = gagg_own[...].reshape(NB_DEV, HB, COLS)
    gagg[:, pl.ds(other, HB), :] = gagg_other[...].reshape(NB_DEV, HB, COLS)
    rel_acc[...] = jnp.zeros_like(rel_acc)
    rel_acc[R8 : R8 + H, :] = upd_sum[...]

    def clear(d, carry):
        slot_acc[pl.ds(d * nz, nz)] = jnp.zeros((nz, HB, COLS), F32)
        return carry

    lax.fori_loop(0, nx * ny, clear, 0)
    copy.wait()

    def one_tile(weight, slot, dst, rel):
        back = jnp.dot(weight, gagg[dst], preferred_element_type=F32)
        row = pl.ds(rel, 1)
        slot_acc[slot] = slot_acc[slot] + back * table[row, :]
        terms = jnp.sum(back * rec[slot].astype(F32), axis=0, keepdims=True)
        rel_acc[row, :] = rel_acc[row, :] + terms

    over_tiles(meta, tiles, weights, buffer, w_sems, one_tile)

    def put(d, carry):
        out[d, : nz * HB, :] = slot_acc[pl.ds(d * nz, nz)].reshape(nz * HB, COLS).astype(BF16)
        start = pl.multiple_of(d * chunk, 16)
        out[d, nz * HB : nz * HB + chunk, :] = rel_acc[pl.ds(start, chunk), :].astype(BF16)
        for part in passed:
            out[d, nz * HB + chunk :, :] = part[...].astype(BF16)
        return carry

    lax.fori_loop(0, nx * ny, put, 0)


def backward(dims, chunk, meta, pos, rec_own, w_own, w_other, gagg_own, gagg_other, table, upd_sum,
             passed):
    nx, nz, ny = dims
    slots, tiles = rec_own.shape[0], w_own.shape[0]
    places = 2 * (tiles // GROUP)
    return pl.pallas_call(
        functools.partial(backward_kernel, dims, tiles, chunk),
        out_shape=jax.ShapeDtypeStruct(
            (nx * ny, nz * HB + chunk * (1 + len(passed)), COLS), BF16
        ),
        in_specs=[SMEM_SPEC, SMEM_SPEC] + [ANY_SPEC] * 3 + [VMEM_SPEC] * (4 + len(passed)),
        out_specs=VMEM_SPEC,
        scratch_shapes=[
            pltpu.VMEM((slots, HB, COLS), BF16),
            pltpu.VMEM((places, GROUP, HB, BLK), BF16),
            pltpu.VMEM((slots, HB, COLS), F32),
            pltpu.VMEM((nx * ny * chunk, COLS), F32),
            pltpu.VMEM((NB_DEV, BLK, COLS), BF16),
            pltpu.SemaphoreType.DMA((places,)),
            pltpu.SemaphoreType.DMA((1,)),
        ],
        compiler_params=params(),
        name="backward",
    )(meta, pos, rec_own, w_own, w_other, gagg_own, gagg_other, table, upd_sum, *passed)


def combine_kernel(dims, chunk, pos, sends, arrived, out, *refs):
    acc = refs[-1]
    nx, nz, ny = dims
    z = pos[1]
    nodes = nx * nz * ny
    acc[...] = jnp.zeros_like(acc)
    rel = jnp.zeros((chunk, COLS), F32)
    for s in range(nx * ny):
        sender = (s // ny) * (nz * ny) + z * ny + s % ny
        for owner in range(nz):
            block = sends[lax.rem(z - owner + nz, nz) * nodes + sender]
            acc[owner, block] = acc[owner, block] + arrived[
                s, owner * HB : (owner + 1) * HB, :
            ].astype(F32)
        rel = rel + arrived[s, nz * HB : nz * HB + chunk, :].astype(F32)
        for whole in refs[:-1]:
            whole[s * chunk : (s + 1) * chunk, :] = arrived[s, nz * HB + chunk :, :].astype(F32)
    for owner in range(nz):
        out[owner, :ROWS, :] = acc[owner].reshape(ROWS, COLS).astype(BF16)
        out[owner, ROWS:, :] = rel.astype(BF16)


def combine(dims, chunk, pos, sends, arrived):
    nx, nz, ny = dims
    outs = [jax.ShapeDtypeStruct((nz, ROWS + chunk, COLS), BF16)]
    if arrived.shape[1] > nz * HB + chunk:
        outs.append(jax.ShapeDtypeStruct((nx * ny * chunk, COLS), F32))
    return pl.pallas_call(
        functools.partial(combine_kernel, dims, chunk),
        out_shape=outs,
        in_specs=[SMEM_SPEC, SMEM_SPEC, VMEM_SPEC],
        out_specs=[VMEM_SPEC] * len(outs),
        scratch_shapes=[pltpu.VMEM((nz, NB_DEV, HB, COLS), F32)],
        compiler_params=params(),
        name="combine",
    )(pos, sends, arrived)


def collect_kernel(more, parts, *refs):
    if more:
        aux_hbm, upd_t, block_mask, aux, sem = refs[1], refs[2], refs[3], refs[-2], refs[-1]
        copy = pltpu.make_async_copy(aux_hbm, aux, sem.at[0])
        copy.start()
    total = parts[0].astype(F32)
    for k in range(1, parts.shape[0]):
        total = total + parts[k].astype(F32)
    grad = refs[0][...].astype(F32) + total[:ROWS]
    if more:
        grad_ref, rel_ref, gagg_ref, upd_ref = refs[4:-2]
        copy.wait()
        before_backward(grad, aux[1], aux[0], upd_t[...], block_mask[...], gagg_ref, upd_ref)
    else:
        grad_ref, rel_ref = refs[1:]
    grad_ref[...] = grad
    rel_ref[...] = total[ROWS:]


def collect(chunk, parts, grad, more):
    outs = [jax.ShapeDtypeStruct((ROWS, COLS), F32), jax.ShapeDtypeStruct((chunk, COLS), F32)]
    in_specs = [VMEM_SPEC, VMEM_SPEC]
    scratch = []
    if more:
        outs.append(jax.ShapeDtypeStruct((ROWS, COLS), BF16))
        outs.append(jax.ShapeDtypeStruct((H, COLS), F32))
        in_specs += [HBM_SPEC, VMEM_SPEC, VMEM_SPEC]
        scratch = [pltpu.VMEM((2, ROWS, COLS), F32), pltpu.SemaphoreType.DMA((1,))]
    return pl.pallas_call(
        functools.partial(collect_kernel, bool(more)),
        out_shape=tuple(outs),
        in_specs=in_specs,
        out_specs=(VMEM_SPEC,) * len(outs),
        scratch_shapes=scratch,
        compiler_params=params(),
        name="collect_more" if more else "collect_last",
    )(parts, grad, *more)


def gather_relations(dims, rel):
    count = dims[0] * dims[2]
    copies = jnp.broadcast_to(rel[None], (count,) + rel.shape)
    parts = lax.all_to_all(copies, ("x", "y"), 0, 0, tiled=True)
    return parts.reshape(count * rel.shape[0], COLS)


def project(query_vec, relation, scale_factor):
    flat = relayout(flat_kernel, (Q, WIDE), relation)
    product = jnp.dot(query_vec.T, flat, precision=EXACT_MATMUL)
    return (product[:, : R * H] * scale_factor).astype(BF16)


def update_sum(relation, scale_factor):
    return relation[R8 : R8 + H].reshape(H, Q, H).sum(1) * scale_factor


def shift(value, axis, count, k):
    return lax.ppermute(value, axis, [(s, (s + k) % count) for s in range(count)])


def whole_rows(core, own, other):
    own, other = (v.reshape(NB_DEV, 1, HB, COLS) for v in (own, other))
    low = jnp.where(core == 0, own, other)
    high = jnp.where(core == 0, other, own)
    return jnp.concatenate([low, high], axis=1).reshape(NB_DEV * BLK, COLS)


def body(dims, node_state, send_list, tile_weight, tile_slot, tile_dst, tile_rel, live_groups,
         query_rel, query_head, rel_table, rel_proj, upd_weight, cotangent):
    nx, nz, ny = dims
    nodes = nx * nz * ny
    chunk = -(-REL_ROWS // (nx * ny * 16)) * 16
    x, z, y, core = (lax.axis_index(a) for a in ("x", "z", "y", "c"))
    node = (x * nz + z) * ny + y
    pos = jnp.stack([x, z, y, core]).astype(jnp.int32)
    tiles = tile_weight.shape[2]

    def own_half(rows):
        return lax.dynamic_index_in_dim(
            rows.reshape(NB_DEV, 2, HB, COLS), core, 1, keepdims=False
        ).reshape(ROWS, COLS)

    def swap(value):
        return lax.ppermute(value, "c", SWAP)

    def column_of(rows):
        pieces = [rows] * nz
        ahead = behind = rows
        for k in range(1, nz // 2 + 1):
            ahead = shift(ahead, "z", nz, 1)
            pieces[k] = ahead
            if k < nz - k:
                behind = shift(behind, "z", nz, -1)
                pieces[nz - k] = behind
        return pieces

    state = own_half(node_state)
    listed = jnp.pad(send_list.astype(BF16), ((0, 15), (0, COLS - nodes)))
    column = column_of(jnp.concatenate([state, listed]))

    slot = tile_slot[0, 0]
    slot = ((slot // (nz * ny)) * ny + slot % ny) * nz + (slot // ny) % nz
    live = jnp.broadcast_to(live_groups[0, 0], (tiles,))
    meta = jnp.stack([slot, tile_dst[0, 0], tile_rel[0, 0], live])
    meta = jnp.stack([meta, swap(meta)]).reshape(-1)

    lane_block = jnp.arange(COLS, dtype=jnp.int32) // H
    block_mask = (lane_block[:, None] == lane_block[None, :]).astype(F32)
    upd = [jnp.tile(upd_weight[l], (Q, Q)) * block_mask for l in range(L)]
    upd_t = [u.T for u in upd]
    cot = own_half(cotangent)
    query_vec = query_vectors(rel_table, query_rel)
    first_table = relation_table(query_vec, rel_proj[0])
    weights = tile_weight[0, 0]
    f_other = swap(weights)
    held = (column, meta, upd, upd_t, block_mask, cot, first_table, f_other)
    held = lax.optimization_barrier(held)
    column, meta, upd, upd_t, block_mask, cot, first_table, f_other = held
    sends = jnp.concatenate([p[ROWS : ROWS + 1, :nodes] for p in column])
    sends = sends.astype(jnp.int32).reshape(-1)
    outgoing = provide(dims, pos, sends, column)
    outgoing, later = lax.optimization_barrier((outgoing, pos))
    b_own, b_send = split_weights(later, weights)
    row_ids = node * (NB_DEV * BLK) + (
        jnp.arange(NB_DEV, dtype=jnp.int32)[:, None] * BLK
        + core * HB
        + jnp.arange(HB, dtype=jnp.int32)[None, :]
    ).reshape(ROWS)
    matches = (row_ids[:, None] == query_head[None, :]).astype(F32)
    bound = (matches[:, :, None] * query_vec[None, :, :]).reshape(ROWS, COLS)

    received, tables = [], []
    for l in range(L):
        if l:
            column, b_other = lax.optimization_barrier((column_of(state), b_other))
            outgoing = provide(dims, pos, sends, column)
            outgoing, vectors = lax.optimization_barrier((outgoing, query_vec))
        else:
            table = first_table
        rec_own = lax.all_to_all(outgoing, ("x", "y"), 0, 0, tiled=True)
        if l:
            table = relation_table(vectors, rel_proj[l])
            rec_own, table = lax.optimization_barrier((rec_own, table))
        else:
            rec_own, bound, b_own, b_send = lax.optimization_barrier(
                (rec_own, bound, b_own, b_send)
            )
        tables.append(table)
        rec_own = rec_own.reshape(nodes, HB, COLS)
        received.append(rec_own)
        last = l == L - 1
        more = (cot, upd_t[l], block_mask) if last else ()
        rec_other = swap(rec_own)
        if l == 0:
            rec_other, b_send = lax.optimization_barrier((rec_other, b_send))
            b_other = swap(b_send)
        made = forward(
            last, meta, pos, rec_own, rec_other, weights, f_other, tables[l], bound, upd[l],
            state, more,
        )
        state = made[0]
        if last:
            gagg, upd_sum = made[1:]
        else:
            aux = pltpu.with_memory_space_constraint(made[1], pltpu.HBM)

    grad = cot
    passed = ()
    scale_factor = float(nodes * NB_DEV * BLK) ** (-0.5)
    for l in reversed(range(L)):
        sent = backward(
            dims, chunk, meta, pos, received[l], b_own, b_other, gagg, swap(gagg), tables[l],
            upd_sum, passed,
        )
        arrived = lax.all_to_all(sent, ("x", "y"), 0, 0, tiled=True)
        combined, *whole = combine(dims, chunk, pos, sends, arrived)
        parts = lax.all_to_all(combined, "z", 0, 0, tiled=True)
        if whole:
            relation = whole[0] + swap(whole[0])
            last_proj = project(query_vec, relation, scale_factor)
            last_upd = update_sum(relation, scale_factor)
            parts, last_proj, last_upd = lax.optimization_barrier((parts, last_proj, last_upd))
        more = (aux, upd_t[0], block_mask) if l else ()
        made = collect(chunk, parts, grad, more)
        grad, rel = made[:2]
        if l:
            gagg, upd_sum = made[2:]
        passed = (rel,) if l else ()
    relation = gather_relations(dims, rel + swap(rel))

    proj = jnp.stack([project(query_vec, relation, scale_factor), last_proj])
    upds = jnp.stack([update_sum(relation, scale_factor), last_upd])
    final_state = whole_rows(core, state, swap(state))
    grad_state = whole_rows(core, grad, swap(grad))
    return (
        final_state,
        grad_state,
        proj,
        upds,
    )


def solution(mesh):
    dims = grid_dims(mesh.shape["node"])
    fine = Mesh(mesh.devices.reshape(*dims, 2), ("x", "z", "y", "c"))
    node = ("x", "z", "y")
    return jax.shard_map(
        functools.partial(body, dims),
        mesh=fine,
        in_specs=(
            P(node, None),
            P(node, None),
            P(node, "c", None, None, None),
            P(node, "c", None),
            P(node, "c", None),
            P(node, "c", None),
            P(node, "c"),
            P(),
            P(),
            P(),
            P(),
            P(),
            P(node, None),
        ),
        out_specs=(P(node, None), P(node, None), P(), P()),
        check_vma=False,
    )
```

```python
import functools

import jax
import jax.numpy as jnp
from jax import lax
from jax.experimental import pallas as pl
from jax.experimental.pallas import tpu as pltpu
from jax.sharding import Mesh
from jax.sharding import PartitionSpec as P

H = 32
R = 535
BLK = 128
HB = BLK // 2
Q = 4
L = 2
GROUP = 16
NB_DEV = 4
COLS = Q * H
ROWS = NB_DEV * HB
R8 = 536
REL_ROWS = R8 + H
F32 = jnp.float32
BF16 = jnp.bfloat16
EXACT_MATMUL = lax.Precision.HIGHEST
VMEM_LIMIT = 48 * 1024 * 1024
SWAP = [(0, 1), (1, 0)]
SMEM_SPEC = pl.BlockSpec(memory_space=pltpu.SMEM)
VMEM_SPEC = pl.BlockSpec(memory_space=pltpu.VMEM)
ANY_SPEC = pl.BlockSpec(memory_space=pl.ANY)
HBM_SPEC = pl.BlockSpec(memory_space=pltpu.HBM)
WIDE = R8 * H
RM = BLK // H


def grid_dims(node_count):
    if node_count == 128:
        return (4, 8, 4)
    return (2, node_count // 4, 2)


def params():
    return pltpu.CompilerParams(vmem_limit_bytes=VMEM_LIMIT)


def query_vectors(rel_table, query_rel):
    relation_ids = jnp.arange(R, dtype=jnp.int32)
    picked = (query_rel[:, None] == relation_ids[None, :]).astype(F32)
    return jnp.dot(picked, rel_table, precision=EXACT_MATMUL)


def lanes_of(shape):
    return lax.broadcasted_iota(jnp.int32, shape, 1) // H


def table_kernel(flat, table, rows):
    for j in range(R8 // RM):
        rows[:, j, :] = flat[:, j * BLK : (j + 1) * BLK]
    lane = lanes_of(rows.shape[1:])
    for m in range(RM):
        made = jnp.zeros(rows.shape[1:], F32)
        for q in range(Q):
            made = jnp.where(lane == q, pltpu.roll(rows[q], (q - m) * H % COLS, 1), made)
        table[pl.ds(m, R8 // RM, stride=RM), :] = made[: R8 // RM]


def project_kernel(scale_factor, query_cols, *refs):
    relations, (out, rows) = refs[:L], refs[L:]
    lane = lanes_of(rows.shape[1:])
    count = rows.shape[1]
    for l in range(L):
        for q in range(Q):
            rows[q] = jnp.zeros((count, COLS), F32)
        for m in range(RM):
            read = relations[l][pl.ds(m, count, stride=RM), :]
            for q in range(Q):
                rows[q] = jnp.where(lane == m, pltpu.roll(read, (m - q) * H % COLS, 1), rows[q])
        cols = [
            jnp.broadcast_to(query_cols[:, q : q + 1] * scale_factor, (H, COLS)) for q in range(Q)
        ]
        for j in range(R8 // RM):
            made = cols[0] * rows[0, j : j + 1, :]
            for q in range(1, Q):
                made = made + cols[q] * rows[q, j : j + 1, :]
            width = min(BLK, R * H - j * BLK)
            out[l, :, j * BLK : j * BLK + width] = made[:, :width].astype(BF16)


def relayout(kernel, shape, value):
    return pl.pallas_call(
        kernel,
        out_shape=jax.ShapeDtypeStruct(shape, F32),
        in_specs=[VMEM_SPEC],
        out_specs=VMEM_SPEC,
        scratch_shapes=[pltpu.VMEM((Q, -(-R8 // (8 * RM)) * 8, COLS), F32)],
        compiler_params=params(),
        cost_estimate=pl.CostEstimate(flops=0, bytes_accessed=4 << 20, transcendentals=0),
        name=kernel.__name__,
    )(value)


def relation_table(query_vec, proj):
    flat = jnp.dot(query_vec, proj.astype(F32), precision=EXACT_MATMUL)
    return relayout(table_kernel, (R8, COLS), jnp.pad(flat, ((0, 0), (0, WIDE - R * H))))


def split_kernel(pos, w_ref, keep, send):
    core = pos[3]
    for t in range(w_ref.shape[0]):
        flipped = w_ref[t].T
        low, high = flipped[:HB], flipped[HB:]
        keep[t] = jnp.where(core == 0, low, high)
        send[t] = jnp.where(core == 0, high, low)


def split_weights(pos, weights):
    tiles = weights.shape[0]
    half = jax.ShapeDtypeStruct((tiles, HB, BLK), BF16)
    spec = pl.BlockSpec((GROUP, HB, BLK), lambda g: (g, 0, 0))
    return pl.pallas_call(
        split_kernel,
        out_shape=(half,) * 2,
        grid=(tiles // GROUP,),
        in_specs=[SMEM_SPEC, pl.BlockSpec((GROUP, BLK, BLK), lambda g: (g, 0, 0))],
        out_specs=[spec] * 2,
        compiler_params=params(),
        cost_estimate=pl.CostEstimate(
            flops=0, bytes_accessed=tiles * BLK * BLK * 2 * 2, transcendentals=0
        ),
        name="split_weights",
    )(pos, weights)


def provide_kernel(dims, pos, sends, *refs):
    nx, nz, ny = dims
    column, (out, blocks, sems) = refs[:nz], refs[nz:]
    z = pos[1]
    nodes = nx * nz * ny
    copies = []
    for d in range(nx * ny):
        reader = (d // ny) * (nz * ny) + z * ny + d % ny
        for k in range(nz):
            block = sends[k * nodes + reader]
            start = pl.multiple_of(block * HB, HB)
            blocks[d, lax.rem(z - k + nz, nz)] = column[k][pl.ds(start, HB), :]
        copies.append(pltpu.make_async_copy(blocks.at[d], out.at[d], sems.at[d]))
        copies[-1].start()
    for copy in copies:
        copy.wait()


def provide(dims, pos, sends, column):
    nx, nz, ny = dims
    shape = (nx * ny, nz, HB, COLS)
    return pl.pallas_call(
        functools.partial(provide_kernel, dims),
        out_shape=pltpu.HBM(shape, BF16),
        in_specs=[SMEM_SPEC, SMEM_SPEC] + [VMEM_SPEC] * nz,
        out_specs=HBM_SPEC,
        scratch_shapes=[pltpu.VMEM(shape, BF16), pltpu.SemaphoreType.DMA((nx * ny,))],
        compiler_params=params(),
        name="provide",
    )(pos, sends, *column)


def start_weights(meta, tiles, weights, buffer, sems):
    groups = tiles // GROUP
    for source in range(2):
        live = meta[(source * 4 + 3) * tiles]
        for g in range(groups):

            @pl.when(g < live)
            def _(source=source, g=g):
                pltpu.make_async_copy(
                    weights[source](pl.ds(g * GROUP, GROUP)),
                    buffer.at[source * groups + g],
                    sems.at[source * groups + g],
                ).start()


def over_tiles(meta, tiles, weights, buffer, sems, one_tile):
    groups = tiles // GROUP
    for source in range(2):
        live = meta[(source * 4 + 3) * tiles]
        base = source * 4 * tiles

        def one_group(g, carry, source=source, base=base):
            place = source * groups + g
            pltpu.make_async_copy(
                weights[source](pl.ds(g * GROUP, GROUP)),
                buffer.at[place],
                sems.at[place],
            ).wait()
            for t in range(GROUP):
                at = base + g * GROUP + t
                one_tile(
                    buffer[place, t],
                    meta[at],
                    meta[at + tiles],
                    meta[at + 2 * tiles],
                )
            return carry

        lax.fori_loop(0, live, one_group, 0)


def update_terms(aggregate, grad_pre, block_mask):
    product = jnp.dot(aggregate.T, grad_pre, precision=EXACT_MATMUL, preferred_element_type=F32)
    product = product * block_mask
    total = product[:H]
    for q in range(1, Q):
        total = total + product[q * H : (q + 1) * H]
    return total


def before_backward(grad, pre, aggregate, upd_t, block_mask, gagg_ref, upd_ref):
    sigma = jax.nn.sigmoid(pre)
    grad_pre = grad * (sigma * (1.0 + pre * (1.0 - sigma)))
    gagg_ref[...] = jnp.dot(
        grad_pre, upd_t, precision=EXACT_MATMUL, preferred_element_type=F32
    ).astype(BF16)
    upd_ref[...] = update_terms(aggregate, grad_pre, block_mask)


def forward_kernel(last, tiles, meta, pos, rec_own, rec_other, w_own, w_other, table, bound,
                   upd, state, *refs):
    if last:
        cotangent, upd_t, block_mask = refs[:3]
        next_ref, gagg_ref, upd_ref, rec, buffer, acc, w_sems, r_sems = refs[3:]
    else:
        next_ref, aux_ref, rec, buffer, acc, w_sems, r_sems, aux = refs
    own = pl.multiple_of(pos[3] * HB, HB)
    other = pl.multiple_of((1 - pos[3]) * HB, HB)
    copies = [
        pltpu.make_async_copy(rec_own, rec.at[:, pl.ds(own, HB), :], r_sems.at[0]),
        pltpu.make_async_copy(rec_other, rec.at[:, pl.ds(other, HB), :], r_sems.at[1]),
    ]
    for copy in copies:
        copy.start()
    weights = [lambda g, w=w: w.at[g, pl.ds(own, HB), :] for w in (w_own, w_other)]
    start_weights(meta, tiles, weights, buffer, w_sems)
    acc[...] = jnp.zeros_like(acc)
    for copy in copies:
        copy.wait()

    def one_tile(weight, slot, dst, rel):
        message = jnp.dot(weight, rec[slot], preferred_element_type=F32)
        acc[dst] = acc[dst] + message * table[pl.ds(rel, 1), :]

    over_tiles(meta, tiles, weights, buffer, w_sems, one_tile)
    aggregate = acc[...].reshape(ROWS, COLS) + bound[...]
    pre = jnp.dot(aggregate, upd[...], precision=EXACT_MATMUL, preferred_element_type=F32)
    next_ref[...] = (state[...].astype(F32) + pre * jax.nn.sigmoid(pre)).astype(BF16)
    if last:
        before_backward(
            cotangent[...].astype(F32), pre, aggregate, upd_t[...], block_mask[...],
            gagg_ref, upd_ref,
        )
    else:
        aux[0] = aggregate
        aux[1] = pre
        kept = pltpu.make_async_copy(aux, aux_ref, r_sems.at[2])
        kept.start()
        kept.wait()


def forward(last, meta, pos, rec_own, rec_other, w_own, w_other, table, bound, upd, state, more):
    slots, tiles = rec_own.shape[0], w_own.shape[0]
    places = 2 * (tiles // GROUP)
    rows16 = jax.ShapeDtypeStruct((ROWS, COLS), BF16)
    pair = pltpu.HBM((2, ROWS, COLS), F32)
    if last:
        outs = (rows16, rows16, jax.ShapeDtypeStruct((H, COLS), F32))
    else:
        outs = (rows16, pair)
    return pl.pallas_call(
        functools.partial(forward_kernel, last, tiles),
        out_shape=outs,
        in_specs=[SMEM_SPEC, SMEM_SPEC] + [ANY_SPEC] * 4 + [VMEM_SPEC] * (4 + len(more)),
        out_specs=(VMEM_SPEC,) * 3 if last else (VMEM_SPEC, HBM_SPEC),
        scratch_shapes=[
            pltpu.VMEM((slots, BLK, COLS), BF16),
            pltpu.VMEM((places, GROUP, HB, BLK), BF16),
            pltpu.VMEM((NB_DEV, HB, COLS), F32),
            pltpu.SemaphoreType.DMA((places,)),
            pltpu.SemaphoreType.DMA((3,)),
        ]
        + ([] if last else [pltpu.VMEM((2, ROWS, COLS), F32)]),
        compiler_params=params(),
        name="forward_last" if last else "forward_first",
    )(meta, pos, rec_own, rec_other, w_own, w_other, table, bound, upd, state, *more)


def backward_kernel(dims, tiles, chunk, meta, pos, rec_own, w_own, w_other, gagg_own,
                    gagg_other, table, upd_sum, *refs):
    passed, refs = refs[:-8], refs[-8:]
    out, rec, buffer, slot_acc, rel_acc, gagg, w_sems, r_sem = refs
    nx, nz, ny = dims
    copy = pltpu.make_async_copy(rec_own, rec, r_sem.at[0])
    copy.start()
    weights = (lambda g: w_own.at[g], lambda g: w_other.at[g])
    start_weights(meta, tiles, weights, buffer, w_sems)
    own = pl.multiple_of(pos[3] * HB, HB)
    other = pl.multiple_of((1 - pos[3]) * HB, HB)
    gagg[:, pl.ds(own, HB), :] = gagg_own[...].reshape(NB_DEV, HB, COLS)
    gagg[:, pl.ds(other, HB), :] = gagg_other[...].reshape(NB_DEV, HB, COLS)
    rel_acc[...] = jnp.zeros_like(rel_acc)
    rel_acc[R8 : R8 + H, :] = upd_sum[...]

    def clear(d, carry):
        slot_acc[pl.ds(d * nz, nz)] = jnp.zeros((nz, HB, COLS), F32)
        return carry

    lax.fori_loop(0, nx * ny, clear, 0)
    copy.wait()

    def one_tile(weight, slot, dst, rel):
        back = jnp.dot(weight, gagg[dst], preferred_element_type=F32)
        row = pl.ds(rel, 1)
        slot_acc[slot] = slot_acc[slot] + back * table[row, :]
        terms = jnp.sum(back * rec[slot].astype(F32), axis=0, keepdims=True)
        rel_acc[row, :] = rel_acc[row, :] + terms

    over_tiles(meta, tiles, weights, buffer, w_sems, one_tile)

    def put(d, carry):
        out[d, : nz * HB, :] = slot_acc[pl.ds(d * nz, nz)].reshape(nz * HB, COLS).astype(BF16)
        start = pl.multiple_of(d * chunk, 16)
        out[d, nz * HB : nz * HB + chunk, :] = rel_acc[pl.ds(start, chunk), :].astype(BF16)
        for part in passed:
            out[d, nz * HB + chunk :, :] = part[...].astype(BF16)
        return carry

    lax.fori_loop(0, nx * ny, put, 0)


def backward(dims, chunk, meta, pos, rec_own, w_own, w_other, gagg_own, gagg_other, table, upd_sum,
             passed):
    nx, nz, ny = dims
    slots, tiles = rec_own.shape[0], w_own.shape[0]
    places = 2 * (tiles // GROUP)
    return pl.pallas_call(
        functools.partial(backward_kernel, dims, tiles, chunk),
        out_shape=jax.ShapeDtypeStruct(
            (nx * ny, nz * HB + chunk * (1 + len(passed)), COLS), BF16
        ),
        in_specs=[SMEM_SPEC, SMEM_SPEC] + [ANY_SPEC] * 3 + [VMEM_SPEC] * (4 + len(passed)),
        out_specs=VMEM_SPEC,
        scratch_shapes=[
            pltpu.VMEM((slots, HB, COLS), BF16),
            pltpu.VMEM((places, GROUP, HB, BLK), BF16),
            pltpu.VMEM((slots, HB, COLS), F32),
            pltpu.VMEM((nx * ny * chunk, COLS), F32),
            pltpu.VMEM((NB_DEV, BLK, COLS), BF16),
            pltpu.SemaphoreType.DMA((places,)),
            pltpu.SemaphoreType.DMA((1,)),
        ],
        compiler_params=params(),
        name="backward",
    )(meta, pos, rec_own, w_own, w_other, gagg_own, gagg_other, table, upd_sum, *passed)


def combine_kernel(dims, chunk, pos, sends, arrived, out, *refs):
    acc = refs[-1]
    nx, nz, ny = dims
    z = pos[1]
    nodes = nx * nz * ny
    acc[...] = jnp.zeros_like(acc)
    rel = jnp.zeros((chunk, COLS), F32)
    for s in range(nx * ny):
        sender = (s // ny) * (nz * ny) + z * ny + s % ny
        for owner in range(nz):
            block = sends[lax.rem(z - owner + nz, nz) * nodes + sender]
            acc[owner, block] = acc[owner, block] + arrived[
                s, owner * HB : (owner + 1) * HB, :
            ].astype(F32)
        rel = rel + arrived[s, nz * HB : nz * HB + chunk, :].astype(F32)
        for whole in refs[:-1]:
            whole[s * chunk : (s + 1) * chunk, :] = arrived[s, nz * HB + chunk :, :].astype(F32)
    for owner in range(nz):
        out[owner, :ROWS, :] = acc[owner].reshape(ROWS, COLS).astype(BF16)
        out[owner, ROWS:, :] = rel.astype(BF16)


def combine(dims, chunk, pos, sends, arrived):
    nx, nz, ny = dims
    outs = [jax.ShapeDtypeStruct((nz, ROWS + chunk, COLS), BF16)]
    if arrived.shape[1] > nz * HB + chunk:
        outs.append(jax.ShapeDtypeStruct((nx * ny * chunk, COLS), F32))
    return pl.pallas_call(
        functools.partial(combine_kernel, dims, chunk),
        out_shape=outs,
        in_specs=[SMEM_SPEC, SMEM_SPEC, VMEM_SPEC],
        out_specs=[VMEM_SPEC] * len(outs),
        scratch_shapes=[pltpu.VMEM((nz, NB_DEV, HB, COLS), F32)],
        compiler_params=params(),
        name="combine",
    )(pos, sends, arrived)


def collect_kernel(more, parts, *refs):
    if more:
        aux_hbm, upd_t, block_mask, aux, sem = refs[1], refs[2], refs[3], refs[-2], refs[-1]
        copy = pltpu.make_async_copy(aux_hbm, aux, sem.at[0])
        copy.start()
    total = parts[0].astype(F32)
    for k in range(1, parts.shape[0]):
        total = total + parts[k].astype(F32)
    grad = refs[0][...].astype(F32) + total[:ROWS]
    if more:
        grad_ref, rel_ref, gagg_ref, upd_ref = refs[4:-2]
        copy.wait()
        before_backward(grad, aux[1], aux[0], upd_t[...], block_mask[...], gagg_ref, upd_ref)
    else:
        grad_ref, rel_ref = refs[1:]
    grad_ref[...] = grad
    rel_ref[...] = total[ROWS:]


def collect(chunk, parts, grad, more):
    outs = [jax.ShapeDtypeStruct((ROWS, COLS), F32), jax.ShapeDtypeStruct((chunk, COLS), F32)]
    in_specs = [VMEM_SPEC, VMEM_SPEC]
    scratch = []
    if more:
        outs.append(jax.ShapeDtypeStruct((ROWS, COLS), BF16))
        outs.append(jax.ShapeDtypeStruct((H, COLS), F32))
        in_specs += [HBM_SPEC, VMEM_SPEC, VMEM_SPEC]
        scratch = [pltpu.VMEM((2, ROWS, COLS), F32), pltpu.SemaphoreType.DMA((1,))]
    return pl.pallas_call(
        functools.partial(collect_kernel, bool(more)),
        out_shape=tuple(outs),
        in_specs=in_specs,
        out_specs=(VMEM_SPEC,) * len(outs),
        scratch_shapes=scratch,
        compiler_params=params(),
        name="collect_more" if more else "collect_last",
    )(parts, grad, *more)


def gather_relations(dims, rel):
    count = dims[0] * dims[2]
    copies = jnp.broadcast_to(rel[None], (count,) + rel.shape)
    parts = lax.all_to_all(copies, ("x", "y"), 0, 0, tiled=True)
    return parts.reshape(count * rel.shape[0], COLS)


def project(query_vec, relations, scale_factor):
    return pl.pallas_call(
        functools.partial(project_kernel, scale_factor),
        out_shape=jax.ShapeDtypeStruct((L, H, R * H), BF16),
        in_specs=[VMEM_SPEC] * (1 + L),
        out_specs=VMEM_SPEC,
        scratch_shapes=[pltpu.VMEM((Q, -(-R8 // (8 * RM)) * 8, COLS), F32)],
        compiler_params=params(),
        name="project",
    )(query_vec.T, *relations)


def update_sum(relation, scale_factor):
    return relation[R8 : R8 + H].reshape(H, Q, H).sum(1) * scale_factor


def shift(value, axis, count, k):
    return lax.ppermute(value, axis, [(s, (s + k) % count) for s in range(count)])


def whole_rows(core, own, other):
    own, other = (v.reshape(NB_DEV, 1, HB, COLS) for v in (own, other))
    low = jnp.where(core == 0, own, other)
    high = jnp.where(core == 0, other, own)
    return jnp.concatenate([low, high], axis=1).reshape(NB_DEV * BLK, COLS)


def body(dims, node_state, send_list, tile_weight, tile_slot, tile_dst, tile_rel, live_groups,
         query_rel, query_head, rel_table, rel_proj, upd_weight, cotangent):
    nx, nz, ny = dims
    nodes = nx * nz * ny
    chunk = -(-REL_ROWS // (nx * ny * 16)) * 16
    x, z, y, core = (lax.axis_index(a) for a in ("x", "z", "y", "c"))
    node = (x * nz + z) * ny + y
    pos = jnp.stack([x, z, y, core]).astype(jnp.int32)
    tiles = tile_weight.shape[2]

    def own_half(rows):
        return lax.dynamic_index_in_dim(
            rows.reshape(NB_DEV, 2, HB, COLS), core, 1, keepdims=False
        ).reshape(ROWS, COLS)

    def swap(value):
        return lax.ppermute(value, "c", SWAP)

    def column_of(rows):
        pieces = [rows] * nz
        ahead = behind = rows
        for k in range(1, nz // 2 + 1):
            ahead = shift(ahead, "z", nz, 1)
            pieces[k] = ahead
            if k < nz - k:
                behind = shift(behind, "z", nz, -1)
                pieces[nz - k] = behind
        return pieces

    state = own_half(node_state)
    listed = jnp.pad(send_list.astype(BF16), ((0, 15), (0, COLS - nodes)))
    column = column_of(jnp.concatenate([state, listed]))

    slot = tile_slot[0, 0]
    slot = ((slot // (nz * ny)) * ny + slot % ny) * nz + (slot // ny) % nz
    live = jnp.broadcast_to(live_groups[0, 0], (tiles,))
    meta = jnp.stack([slot, tile_dst[0, 0], tile_rel[0, 0], live])
    meta = jnp.stack([meta, swap(meta)]).reshape(-1)

    lane_block = jnp.arange(COLS, dtype=jnp.int32) // H
    block_mask = (lane_block[:, None] == lane_block[None, :]).astype(F32)
    upd = [jnp.tile(upd_weight[l], (Q, Q)) * block_mask for l in range(L)]
    upd_t = [u.T for u in upd]
    cot = own_half(cotangent)
    weights = tile_weight[0, 0]
    f_other = swap(weights)
    held = (column, meta, upd, upd_t, block_mask, cot, f_other)
    held = lax.optimization_barrier(held)
    column, meta, upd, upd_t, block_mask, cot, f_other = held
    sends = jnp.concatenate([p[ROWS : ROWS + 1, :nodes] for p in column])
    sends = sends.astype(jnp.int32).reshape(-1)
    outgoing = provide(dims, pos, sends, column)
    outgoing, later, query_rel = lax.optimization_barrier((outgoing, pos, query_rel))
    query_vec = query_vectors(rel_table, query_rel)
    first_table = relation_table(query_vec, rel_proj[0])
    b_own, b_send = split_weights(later, weights)
    row_ids = node * (NB_DEV * BLK) + (
        jnp.arange(NB_DEV, dtype=jnp.int32)[:, None] * BLK
        + core * HB
        + jnp.arange(HB, dtype=jnp.int32)[None, :]
    ).reshape(ROWS)
    matches = (row_ids[:, None] == query_head[None, :]).astype(F32)
    bound = (matches[:, :, None] * query_vec[None, :, :]).reshape(ROWS, COLS)

    received, tables = [], []
    for l in range(L):
        if l:
            column, b_other = lax.optimization_barrier((column_of(state), b_other))
            outgoing = provide(dims, pos, sends, column)
            outgoing, vectors = lax.optimization_barrier((outgoing, query_vec))
        else:
            table = first_table
        rec_own = lax.all_to_all(outgoing, ("x", "y"), 0, 0, tiled=True)
        if l:
            table = relation_table(vectors, rel_proj[l])
            rec_own, table = lax.optimization_barrier((rec_own, table))
        else:
            rec_own, bound, b_own, b_send, table = lax.optimization_barrier(
                (rec_own, bound, b_own, b_send, table)
            )
        tables.append(table)
        rec_own = rec_own.reshape(nodes, HB, COLS)
        received.append(rec_own)
        last = l == L - 1
        more = (cot, upd_t[l], block_mask) if last else ()
        rec_other = swap(rec_own)
        if l == 0:
            rec_other, b_send = lax.optimization_barrier((rec_other, b_send))
            b_other = swap(b_send)
        made = forward(
            last, meta, pos, rec_own, rec_other, weights, f_other, tables[l], bound, upd[l],
            state, more,
        )
        state = made[0]
        if last:
            gagg, upd_sum = made[1:]
        else:
            aux = pltpu.with_memory_space_constraint(made[1], pltpu.HBM)

    grad = cot
    passed = ()
    scale_factor = float(nodes * NB_DEV * BLK) ** (-0.5)
    for l in reversed(range(L)):
        sent = backward(
            dims, chunk, meta, pos, received[l], b_own, b_other, gagg, swap(gagg), tables[l],
            upd_sum, passed,
        )
        arrived = lax.all_to_all(sent, ("x", "y"), 0, 0, tiled=True)
        combined, *whole = combine(dims, chunk, pos, sends, arrived)
        parts = lax.all_to_all(combined, "z", 0, 0, tiled=True)
        if whole:
            relation = whole[0] + swap(whole[0])
            last_upd = update_sum(relation, scale_factor)
            parts, last_relation, last_upd = lax.optimization_barrier((parts, relation, last_upd))
        more = (aux, upd_t[0], block_mask) if l else ()
        made = collect(chunk, parts, grad, more)
        grad, rel = made[:2]
        if l:
            gagg, upd_sum = made[2:]
        passed = (rel,) if l else ()
    relation = gather_relations(dims, rel + swap(rel))

    proj = project(query_vec, [relation, last_relation], scale_factor)
    upds = jnp.stack([update_sum(relation, scale_factor), last_upd])
    final_state = whole_rows(core, state, swap(state))
    grad_state = whole_rows(core, grad, swap(grad))
    return (
        final_state,
        grad_state,
        proj,
        upds,
    )


def solution(mesh):
    dims = grid_dims(mesh.shape["node"])
    fine = Mesh(mesh.devices.reshape(*dims, 2), ("x", "z", "y", "c"))
    node = ("x", "z", "y")
    return jax.shard_map(
        functools.partial(body, dims),
        mesh=fine,
        in_specs=(
            P(node, None),
            P(node, None),
            P(node, "c", None, None, None),
            P(node, "c", None),
            P(node, "c", None),
            P(node, "c", None),
            P(node, "c"),
            P(),
            P(),
            P(),
            P(),
            P(),
            P(node, None),
        ),
        out_specs=(P(node, None), P(node, None), P(), P()),
        check_vma=False,
    )
```
